32 devices in a mesh: dom: 16 (over z, y, x), chan: 2 (over core).
Axes of the slice: x: 2, y: 2, z: 4, core: 2. Of those that a mesh axis runs over, the one named last changes fastest.
Arguments:
- features: bfloat16 [16384, 512], P('dom', 'chan'), may hold values from -6 to 6
- w_self: bfloat16 [512, 512], P('chan'), may hold values from -0.25 to 0.25
- w_neigh: bfloat16 [512, 512], P('chan'), may hold values from -1.5 to 1.5
- degrees: int32 [16384], P('dom'), may hold values from 16 to 48
- local_src: int32 [128], P('dom'), may hold values from 0 to 7
- local_dst: int32 [128], P('dom'), may hold values from 0 to 7
- local_tiles: bfloat16 [128, 128, 128], P('dom'), may hold values from 0 to 1, as said below
- remote_src: int32 [256], P('dom'), may hold values from 0 to 7
- remote_part: int32 [256, 1], P('dom'), may hold values from 0 to 15; in each aligned block of 16 rows (0 to 15, 16 to 31, ...) at most 2 rows name the same one
- remote_dst: int32 [256], P('dom'), may hold values from 0 to 7
- remote_tiles: bfloat16 [256, 128, 128], P('dom'), may hold values from 0 to 1, as said below
- cotangent: bfloat16 [16384, 512], P('dom', 'chan'), may hold values from -6 to 6
Outputs:
- output: bfloat16 [16384, 512], P('dom', 'chan')
- grad_self: float32 [512, 512], P('chan')
- grad_neigh: float32 [512, 512], P('chan')
- grad_features: bfloat16 [16384, 512], P('dom', 'chan')
The draws below stay inside these ranges and needn't reach their ends.
Inputs may be any that keep to these rules, and one draw needn't show every extreme that they name: `remote_part`: among the 16 remote tiles of one partition each partition is named at most 2 times, a bound that some block reaches. `local_tiles`: every entry is 0 or 1. `remote_tiles`: every entry is 0 or 1.
All inputs are finite; a program needn't handle non-finite values.
Results may differ from the reference program's by a relative error of at most 0.015.
Values may be sent and summed in bfloat16 or wider, within the bound.
No kernel may reach another device: no remote copies, remote signals or barrier semaphores. Data moves between devices by JAX's collectives and lax.ppermute only.
A program may use at most 64 MiB of HBM per device.

```python
import math
import jax
import jax.numpy as jnp
import numpy as np
from jax import lax

F = 512
F_OUT = 512
TILE = 128
CAP = 2
BLK_DEV = 8
LOCAL = 8
REMOTE = 16
NODES = 16384
BLOCKS = 128
N_DOM = 16
N_CHAN = 2


def draw_local_tiles(key, part):
    picks = jax.random.uniform(key, (N_DOM * LOCAL, TILE, TILE), jnp.float32)
    return jnp.where(picks < 0.0625, 1.0, 0.0).astype(jnp.float32).astype(jnp.bfloat16)


def draw_remote_tiles(key, part):
    picks = jax.random.uniform(key, (N_DOM * REMOTE, TILE, TILE), jnp.float32)
    return jnp.where(picks < 0.0625, 1.0, 0.0).astype(jnp.float32).astype(jnp.bfloat16)


def place_ends(values, key, smallest, high):
    extent = values.shape
    index_at = [jax.random.randint(jax.random.fold_in(key, axis), (), 0, extent[axis]) for axis in range(len(extent))]
    values = values.at[tuple(index_at)].set(smallest)
    longest = extent.index(max(extent))
    index_at[longest] = (index_at[longest] + 1) % extent[longest]
    return values.at[tuple(index_at)].set(high)


def level_of(stream_key, shape, shards, smallest, largest):
    def one(axis_at, blocks):
        steps = jax.random.uniform(jax.random.fold_in(jax.random.fold_in(stream_key, 6), axis_at), (blocks,), jnp.float32, smallest / len(shards), largest / len(shards))
        return jnp.repeat(jnp.exp(steps), shape[axis_at] // blocks).reshape((-1,) + (1,) * (len(shape) - axis_at - 1))

    gain = one(*shards[0])
    for cut in shards[1:]:
        gain = gain * one(*cut)
    return gain


def routed_block(key, own, number, rows, count, top, most, skew):
    ranking = jax.random.permutation(key, count)
    crowded, ordinary = portions_of(count, rows * top, most, skew, True), portions_of(count, rows * top, most, skew, False)
    places = jnp.arange(count)

    def named(sizes, offset_by):
        used = int((sizes > 0).sum())
        fixed = max(1, used // 4)
        moved = fixed + (places - fixed + offset_by * (used - fixed)) % max(1, count - fixed)
        return jnp.zeros((count,), jnp.int32).at[ranking[jnp.where(places < fixed, places, moved)]].set(jnp.asarray(sizes, jnp.int32))

    sizes = jnp.where(number % 4 == 0, named(crowded, number // 4), named(ordinary, number - number // 4 - 1))
    mixed = jax.random.permutation(jax.random.fold_in(own, 3), count)
    giver, taker = mixed[0:count // 2 * 2:2], mixed[1:count // 2 * 2:2]
    slack = jnp.minimum(sizes[giver] - 1, most - sizes[taker]) // 2
    slack = jnp.where((giver == ranking[0]) | (taker == ranking[0]) | (sizes[taker] == 0), 0, jnp.maximum(slack, 0))
    moved = jax.random.randint(jax.random.fold_in(own, 4), (count // 2,), 0, 1 << 20) % (slack + 1)
    sizes = sizes.at[giver].add(-moved).at[taker].add(moved)
    items = jnp.searchsorted(jnp.cumsum(sizes), jnp.arange(rows * top), side="right").astype(jnp.int32)
    table = items.reshape(top, rows).T
    table = table[jax.random.permutation(jax.random.fold_in(own, 1), rows)]
    offset_by = jax.random.randint(jax.random.fold_in(own, 2), (rows, 1), 0, top)
    return jnp.take_along_axis(table, (jnp.arange(top)[None, :] + offset_by) % top, axis=1)


def portions_of(number_of, total, limit, slope, full):
    portions = [(1 << 20) // math.isqrt(grade ** slope) + 1 for grade in range(1, number_of + 1)]
    largest = limit if full else min(limit, max(-(-total // number_of), total * portions[0] // sum(portions)))
    least = 1 if total - largest >= number_of - 1 else 0
    holding, spare = [largest] + [least] * (number_of - 1), total - largest - least * (number_of - 1)
    while spare > 0:
        candidates = [i for i in range(1, number_of) if holding[i] < largest] or [i for i in range(1, number_of) if holding[i] < limit]
        pool, left = sum([portions[i] for i in candidates]), spare
        for i in candidates:
            more = min(limit - holding[i], max(1, left * portions[i] // pool), spare)
            holding[i] = holding[i] + more
            spare = spare - more
    return np.array(holding)


def normal_values(rng, extent, width, limit, split=(), kind=jnp.bfloat16):
    entries = jax.random.normal(rng, extent, jnp.float32) * width
    if len(split) > 0:
        entries = level_of(rng, extent, split, -0.22, 0.18) * entries
    return jnp.clip(entries, min=-limit, max=limit).astype(kind)


def setup_inputs(seed: int = 0) -> dict:
    streams_of = jax.random.split(jax.random.key(seed), 13)
    features = normal_values(streams_of[0], (NODES, F), 1.0, 6.0, ((0, 16), (1, 2)))
    w_self = normal_values(streams_of[1], (F, F_OUT), F ** -0.5, 0.25, ((0, 2),))
    w_neigh = normal_values(streams_of[2], (F, F_OUT), (F // 32) ** -0.5, 1.5, ((0, 2),))
    degrees = place_ends(jax.random.randint(streams_of[3], (NODES,), 16, 49), jax.random.fold_in(streams_of[3], 1), 16, 48).astype(jnp.int32)
    local_src = place_ends(jax.random.randint(streams_of[4], (N_DOM * LOCAL,), 0, BLK_DEV), jax.random.fold_in(streams_of[4], 1), 0, BLK_DEV - 1).astype(jnp.int32)
    local_dst = place_ends(jax.random.randint(streams_of[5], (N_DOM * LOCAL,), 0, BLK_DEV), jax.random.fold_in(streams_of[5], 1), 0, BLK_DEV - 1).astype(jnp.int32)
    local_tiles = draw_local_tiles(jax.random.fold_in(streams_of[12], 71), 0)
    remote_src = place_ends(jax.random.randint(streams_of[7], (N_DOM * REMOTE,), 0, BLK_DEV), jax.random.fold_in(streams_of[7], 1), 0, BLK_DEV - 1).astype(jnp.int32)
    remote_part_keys = jax.random.split(jax.random.fold_in(streams_of[8], 1), (N_DOM * REMOTE) // REMOTE)
    remote_part_turns = jax.random.permutation(jax.random.fold_in(streams_of[8], 3), (N_DOM * REMOTE) // REMOTE)
    remote_part = jax.vmap(lambda own, number: routed_block(jax.random.fold_in(streams_of[8], 2), own, number, REMOTE, N_DOM, 1, CAP, 2))(remote_part_keys, remote_part_turns).reshape((N_DOM * REMOTE, 1))
    remote_dst = place_ends(jax.random.randint(streams_of[9], (N_DOM * REMOTE,), 0, BLK_DEV), jax.random.fold_in(streams_of[9], 1), 0, BLK_DEV - 1).astype(jnp.int32)
    remote_tiles = draw_remote_tiles(jax.random.fold_in(streams_of[12], 71), 0)
    cotangent = normal_values(streams_of[11], (NODES, F_OUT), 1.0, 6.0, ((0, 16), (1, 2)))
    return {"features": features, "w_self": w_self, "w_neigh": w_neigh, "degrees": degrees, "local_src": local_src, "local_dst": local_dst, "local_tiles": local_tiles, "remote_src": remote_src, "remote_part": remote_part, "remote_dst": remote_dst, "remote_tiles": remote_tiles, "cotangent": cotangent}


def silu_slope(value):
    sig = jax.nn.sigmoid(value)
    return sig * (1.0 + value * (1.0 - sig))

def reference(features, w_self, w_neigh, degrees, local_src, local_dst, local_tiles, remote_src, remote_part, remote_dst, remote_tiles, cotangent):
    channels = F // N_CHAN
    feat_blocks = features.reshape(BLOCKS, TILE, F)
    local_owner = jnp.arange(N_DOM * LOCAL, dtype=jnp.int32) // LOCAL * BLK_DEV
    local_from = (local_owner + local_src).astype(jnp.int32)
    local_into = (local_owner + local_dst).astype(jnp.int32)
    remote_owner = jnp.arange(N_DOM * REMOTE, dtype=jnp.int32) // REMOTE * BLK_DEV
    remote_from = (remote_owner + remote_src).astype(jnp.int32)
    remote_into = (remote_part[:, 0] * BLK_DEV + remote_dst).astype(jnp.int32)

    def add_local(summed, tile_item):
        tile_value, source, target = tile_item
        term = jnp.dot(tile_value.T, feat_blocks[source], preferred_element_type=jnp.float32)
        return (summed.at[target].add(term), None)

    def add_remote(summed, tile_item):
        tile_value, source, target = tile_item
        term = jnp.dot(tile_value.T, feat_blocks[source], preferred_element_type=jnp.float32)
        term = term.astype(jnp.bfloat16).astype(jnp.float32)
        return (summed.at[target].add(term), None)
    summed = jnp.zeros((BLOCKS, TILE, F), jnp.float32)
    summed, _ = lax.scan(add_local, summed, (local_tiles, local_from, local_into))
    summed, _ = lax.scan(add_remote, summed, (remote_tiles, remote_from, remote_into))
    divisor = degrees.astype(jnp.float32)[:, None]
    averaged = (summed.reshape(NODES, F) / divisor).astype(jnp.bfloat16)
    preact = jnp.zeros((NODES, F_OUT), jnp.float32)
    for chan_shard in range(N_CHAN):
        low = chan_shard * channels
        high = low + channels
        share = jnp.dot(features[:, low:high], w_self[low:high], preferred_element_type=jnp.float32)
        share = share + jnp.dot(averaged[:, low:high], w_neigh[low:high], preferred_element_type=jnp.float32)
        preact = preact + share.astype(jnp.bfloat16).astype(jnp.float32)
    output = jax.nn.silu(preact).astype(jnp.bfloat16)
    slopes = (cotangent.astype(jnp.float32) * silu_slope(preact)).astype(jnp.bfloat16)
    scale = 1.0 / math.sqrt(float(NODES))
    grad_self = jnp.dot(features.T, slopes, preferred_element_type=jnp.float32) * scale
    grad_neigh = jnp.dot(averaged.T, slopes, preferred_element_type=jnp.float32) * scale
    back_self = jnp.dot(slopes, w_self.T, preferred_element_type=jnp.float32)
    back_rows = (jnp.dot(slopes, w_neigh.T, preferred_element_type=jnp.float32) / divisor).astype(jnp.bfloat16)
    back_blocks = back_rows.reshape(BLOCKS, TILE, F)

    def add_back(gathered, tile_item):
        tile_value, source, target = tile_item
        term = jnp.dot(tile_value, back_blocks[target], preferred_element_type=jnp.float32)
        return (gathered.at[source].add(term), None)
    gathered = jnp.zeros((BLOCKS, TILE, F), jnp.float32)
    gathered, _ = lax.scan(add_back, gathered, (local_tiles, local_from, local_into))
    gathered, _ = lax.scan(add_back, gathered, (remote_tiles, remote_from, remote_into))
    grad_features = (back_self + gathered.reshape(NODES, F)).astype(jnp.bfloat16)
    return (output, grad_self, grad_neigh, grad_features)
```

```python
import math

import jax
import jax.numpy as jnp
from jax import lax
from jax.experimental import pallas as pl
from jax.experimental.pallas import tpu as pltpu
from jax.sharding import PartitionSpec as P

TILE = 128
CAP = 2
TAG_ROWS = 8
TAG_BITS = 4
TAGS_PER_WORD = 3

F32 = jnp.float32
BF16 = jnp.bfloat16
VMEM = pl.BlockSpec(memory_space=pltpu.VMEM)
SMEM = pl.BlockSpec(memory_space=pltpu.SMEM)


def call(kernel, name, out_shape, in_specs, out_specs, scratch, flops, nbytes):
    return pl.pallas_call(
        kernel,
        out_shape=out_shape,
        in_specs=in_specs,
        out_specs=out_specs,
        scratch_shapes=scratch,
        name=name,
        compiler_params=pltpu.CompilerParams(vmem_limit_bytes=24 * 1024 * 1024),
        cost_estimate=pl.CostEstimate(flops=flops, bytes_accessed=nbytes, transcendentals=0),
    )


def dot_tn(a, b):
    return lax.dot_general(a, b, (((0,), (0,)), ((), ())), preferred_element_type=F32)


def dot_nn(a, b):
    return lax.dot_general(a, b, (((1,), (0,)), ((), ())), preferred_element_type=F32)


def dot_nt(a, b):
    return lax.dot_general(a, b, (((1,), (1,)), ((), ())), preferred_element_type=F32)


def clear_counts(count):
    for place in range(count.shape[0]):
        count[place] = 0


def next_slot(part, count, number):
    target = part[number]
    place = count[target]
    count[target] = place + 1
    return target, place


def push_kernel(src, part, dst, feat, tiles, out, count):
    clear_counts(count)
    rows = out.shape[1] - TAG_ROWS
    out[:, rows:, :] = jnp.zeros((out.shape[0], TAG_ROWS, out.shape[2]), BF16)
    row_at = lax.broadcasted_iota(jnp.int32, (TAG_ROWS, out.shape[2]), 0)
    for number in range(tiles.shape[0]):
        target, place = next_slot(part, count, number)
        product = dot_tn(tiles[number], feat[src[number]])
        start = pl.multiple_of(place * TILE, TILE)
        out[target, pl.ds(start, TILE), :] = product.astype(BF16)
        tag = (dst[number] + 1).astype(F32)
        old = out[target, rows:, :].astype(F32)
        out[target, rows:, :] = jnp.where(row_at == place, tag, old).astype(BF16)


def local_kernel(src, dst, feat, tiles, out):
    out[...] = jnp.zeros(out.shape, F32)
    for number in range(tiles.shape[0]):
        out[dst[number]] += dot_tn(tiles[number], feat[src[number]])


def read_tags(recv, got):
    domains = recv.shape[0]
    rows = recv.shape[1] - TAG_ROWS
    row_at = lax.broadcasted_iota(jnp.int32, (TAG_ROWS, recv.shape[2]), 0)
    unit = jnp.where(row_at == 0, 1.0, 0.0)
    for place in range(1, CAP):
        unit = jnp.where(row_at == place, float(1 << (TAG_BITS * place)), unit)
    width = TAG_BITS * CAP
    for first in range(0, domains, TAGS_PER_WORD):
        members = range(first, min(first + TAGS_PER_WORD, domains))
        word = jnp.zeros((TAG_ROWS, recv.shape[2]), F32)
        for member in members:
            scale = float(1 << (width * (member - first)))
            word = word + recv[member, rows:, :].astype(F32) * (unit * scale)
        packed = jnp.max(jnp.sum(word, axis=0, keepdims=True)).astype(jnp.int32)
        for member in members:
            for place in range(CAP):
                shift = width * (member - first) + TAG_BITS * place
                got[member * CAP + place] = ((packed >> shift) & (2**TAG_BITS - 1)) - 1


def mid_kernel(recv, local, feat, w_self, w_neigh, degrees, averaged, share, got, acc):
    read_tags(recv, got)
    acc[...] = local[...]
    for slot in range(recv.shape[0] * CAP):
        block = got[slot]

        @pl.when(block >= 0)
        def _():
            start = (slot % CAP) * TILE
            acc[block] += recv[slot // CAP, start : start + TILE, :].astype(F32)

    width = share.shape[2]
    for block in range(acc.shape[0]):
        at = slice(block * TILE, (block + 1) * TILE)
        mean = (acc[block] / degrees[at, :]).astype(BF16)
        averaged[at, :] = mean
        value = dot_nn(feat[block], w_self[...]) + dot_nn(mean, w_neigh[...])
        value = value.astype(BF16)
        for piece in range(share.shape[0]):
            share[piece, at, :] = value[:, piece * width : (piece + 1) * width]


def silu_kernel(*refs):
    shares, cotangent, output, slopes = refs[:-3], refs[-3], refs[-2], refs[-1]
    step = TILE
    for start in range(0, output.shape[0], step):
        at = slice(start, start + step)
        value = shares[0][at, :].astype(F32)
        for piece in shares[1:]:
            value = value + piece[at, :].astype(F32)
        gate = 1.0 / (1.0 + jnp.exp(-value))
        output[at, :] = (value * gate).astype(BF16)
        slope = gate * (1.0 + value * (1.0 - gate))
        slopes[at, :] = (cotangent[at, :].astype(F32) * slope).astype(BF16)


def back_kernel(*refs):
    got, w_neigh, degrees = refs[:3]
    slopes, back, returning = refs[3:-2], refs[-2], refs[-1]
    width = slopes[0].shape[1]
    for block in range(back.shape[0]):
        at = slice(block * TILE, (block + 1) * TILE)
        total = dot_nt(slopes[0][at, :], w_neigh[:, :width])
        for piece in range(1, len(slopes)):
            columns = slice(piece * width, (piece + 1) * width)
            total = total + dot_nt(slopes[piece][at, :], w_neigh[:, columns])
        back[block] = (total / degrees[at, :]).astype(BF16)
    for slot in range(returning.shape[0] * CAP):
        block = got[slot]

        @pl.when(block >= 0)
        def _():
            start = (slot % CAP) * TILE
            returning[slot // CAP, start : start + TILE, :] = back[block]


def grads_kernel(*refs):
    feat, averaged, slopes, out = refs[0], refs[1], refs[2:-1], refs[-1]
    channels = feat.shape[1]
    width = slopes[0].shape[1]
    for piece, slope in enumerate(slopes):
        columns = slice(piece * width, (piece + 1) * width)
        out[:channels, columns] = dot_tn(feat[...], slope[...])
        out[channels:, columns] = dot_tn(averaged[...], slope[...])


def local_back_kernel(*refs):
    src, dst, tiles, back, w_self = refs[:5]
    slopes, out = refs[5:-1], refs[-1]
    width = slopes[0].shape[1]
    for block in range(out.shape[0]):
        at = slice(block * TILE, (block + 1) * TILE)
        total = dot_nt(slopes[0][at, :], w_self[:, :width])
        for piece in range(1, len(slopes)):
            columns = slice(piece * width, (piece + 1) * width)
            total = total + dot_nt(slopes[piece][at, :], w_self[:, columns])
        out[block] = total
    for number in range(tiles.shape[0]):
        out[src[number]] += dot_nn(tiles[number], back[dst[number]])


def final_kernel(src, part, tiles, returned, partial, out, count, acc):
    clear_counts(count)
    acc[...] = partial[...]
    for number in range(tiles.shape[0]):
        target, place = next_slot(part, count, number)
        start = pl.multiple_of(place * TILE, TILE)
        acc[src[number]] += dot_nn(tiles[number], returned[target, pl.ds(start, TILE), :])
    for block in range(acc.shape[0]):
        out[block] = acc[block].astype(BF16)


def shift_pairs(count, shift):
    return [(at, (at + shift) % count) for at in range(count)]


def reduce_over(value, axis):
    count = lax.axis_size(axis)
    here = lax.axis_index(axis)
    bits = count.bit_length() - 1
    rows, columns = value.shape
    sizes = []
    for bit in range(bits):
        half = value.shape[0] // 2
        upper = (here >> bit) & 1
        low, high = value[:half], value[half:]
        keep = jnp.where(upper == 1, high, low)
        send = jnp.where(upper == 1, low, high).astype(BF16)
        pairs = [(at, at ^ (1 << bit)) for at in range(count)]
        arrived = lax.ppermute(send, axis, pairs)
        value = keep + arrived.astype(F32)
    value = value.astype(BF16)
    for bit in reversed(range(bits)):
        upper = (here >> bit) & 1
        pairs = [(at, at ^ (1 << bit)) for at in range(count)]
        arrived = lax.ppermute(value, axis, pairs)
        low = jnp.where(upper == 1, arrived, value)
        high = jnp.where(upper == 1, value, arrived)
        value = jnp.concatenate([low, high], axis=0)
    return value.astype(F32)


def rotate_columns(weights, pieces, me):
    rows, columns = weights.shape
    double = jnp.concatenate([weights, weights], axis=1)
    return lax.dynamic_slice(double, (0, me * (columns // pieces)), (rows, columns))


def per_device(
    features,
    w_self,
    w_neigh,
    degrees,
    local_src,
    local_dst,
    local_tiles,
    remote_src,
    remote_part,
    remote_dst,
    remote_tiles,
    cotangent,
):
    domains = lax.axis_size("dom")
    shards = lax.axis_size("chan")
    me = lax.axis_index("chan")
    node_rows, channels = features.shape
    out_width = w_self.shape[1]
    own_width = out_width // shards
    blocks = node_rows // TILE
    rows = CAP * TILE
    n_remote, n_local = remote_tiles.shape[0], local_tiles.shape[0]
    feat_blocks = features.reshape(blocks, TILE, channels)
    targets = remote_part[:, 0]
    shape = jax.ShapeDtypeStruct
    tile_flops = 2 * TILE * TILE * channels
    block_bytes = 2 * TILE * channels

    outgoing = call(
        push_kernel,
        "push",
        shape((domains, rows + TAG_ROWS, channels), BF16),
        [SMEM, SMEM, SMEM, VMEM, VMEM],
        VMEM,
        [pltpu.SMEM((domains,), jnp.int32)],
        n_remote * tile_flops,
        (blocks + domains * CAP) * block_bytes,
    )(remote_src, targets, remote_dst, feat_blocks, remote_tiles)
    received = lax.all_to_all(outgoing, "dom", split_axis=0, concat_axis=0, tiled=True)

    local = call(
        local_kernel,
        "local",
        shape((blocks, TILE, channels), F32),
        [SMEM, SMEM, VMEM, VMEM],
        VMEM,
        [],
        n_local * tile_flops,
        3 * blocks * block_bytes,
    )(local_src, local_dst, feat_blocks, local_tiles)
    divisor = degrees.astype(F32)[:, None]
    own_self = rotate_columns(w_self, shards, me)
    own_neigh = rotate_columns(w_neigh, shards, me)

    averaged, share, got = call(
        mid_kernel,
        "mid",
        (
            shape((node_rows, channels), BF16),
            shape((shards, node_rows, own_width), BF16),
            shape((domains * CAP,), jnp.int32),
        ),
        [VMEM] * 6,
        (VMEM, VMEM, SMEM),
        [pltpu.VMEM((blocks, TILE, channels), F32)],
        4 * node_rows * channels * out_width,
        (domains * CAP + 4 * blocks) * block_bytes,
    )(received, local, feat_blocks, own_self, own_neigh, divisor)

    pieces = [share[0]]
    for shift in range(1, shards):
        pieces.append(lax.ppermute(share[shift], "chan", shift_pairs(shards, shift)))
    output, slopes_own = call(
        silu_kernel,
        "silu",
        (shape((node_rows, own_width), BF16), shape((node_rows, own_width), BF16)),
        [VMEM] * (shards + 1),
        (VMEM, VMEM),
        [],
        20 * node_rows * own_width,
        10 * node_rows * own_width,
    )(*pieces, cotangent)
    slopes = [slopes_own]
    for block in range(1, shards):
        pairs = shift_pairs(shards, shards - block)
        slopes.append(lax.ppermute(slopes_own, "chan", pairs))

    back, returning = call(
        back_kernel,
        "back",
        (shape((blocks, TILE, channels), BF16), shape((domains, rows, channels), BF16)),
        [SMEM, VMEM, VMEM] + [VMEM] * shards,
        (VMEM, VMEM),
        [],
        2 * node_rows * channels * out_width,
        (domains * CAP + 4 * blocks) * block_bytes,
    )(got, own_neigh, divisor, *slopes)
    returned = lax.all_to_all(returning, "dom", split_axis=0, concat_axis=0, tiled=True)

    grad_terms = call(
        grads_kernel,
        "grads",
        shape((2 * channels, out_width), F32),
        [VMEM] * (2 + shards),
        VMEM,
        [],
        4 * node_rows * channels * out_width,
        8 * node_rows * channels,
    )(features, averaged, *slopes)
    scale = 1.0 / math.sqrt(float(node_rows * domains))
    grad_sums = reduce_over(grad_terms, "dom") * scale
    grad_sums = rotate_columns(grad_sums, shards, (shards - me) % shards)

    partial = call(
        local_back_kernel,
        "local_back",
        shape((blocks, TILE, channels), F32),
        [SMEM, SMEM, VMEM, VMEM, VMEM] + [VMEM] * shards,
        VMEM,
        [],
        2 * node_rows * channels * out_width + n_local * tile_flops,
        8 * blocks * block_bytes,
    )(local_src, local_dst, local_tiles, back, own_self, *slopes)
    grad_features = call(
        final_kernel,
        "final",
        shape((blocks, TILE, channels), BF16),
        [SMEM, SMEM, VMEM, VMEM, VMEM],
        VMEM,
        [pltpu.SMEM((domains,), jnp.int32), pltpu.VMEM((blocks, TILE, channels), F32)],
        n_remote * tile_flops,
        (domains * CAP + 4 * blocks) * block_bytes,
    )(remote_src, targets, remote_tiles, returned, partial)
    return (
        output,
        grad_sums[:channels],
        grad_sums[channels:],
        grad_features.reshape(node_rows, channels),
    )


def solution(mesh):
    in_specs = (
        P("dom", "chan"),
        P("chan", None),
        P("chan", None),
        P("dom"),
        P("dom"),
        P("dom"),
        P("dom", None, None),
        P("dom"),
        P("dom", None),
        P("dom"),
        P("dom", None, None),
        P("dom", "chan"),
    )
    out_specs = (P("dom", "chan"), P("chan", None), P("chan", None), P("dom", "chan"))
    return jax.shard_map(
        per_device, mesh=mesh, in_specs=in_specs, out_specs=out_specs, check_vma=False
    )
```

```python
import math

import jax
import jax.numpy as jnp
from jax import lax
from jax.experimental import pallas as pl
from jax.experimental.pallas import tpu as pltpu
from jax.sharding import PartitionSpec as P


TILE = 128
CAP = 2
TAG_ROWS = 8
PAIR = CAP * TILE

F32 = jnp.float32
BF16 = jnp.bfloat16
I32 = jnp.int32
VMEM = pl.BlockSpec(memory_space=pltpu.VMEM)
SMEM = pl.BlockSpec(memory_space=pltpu.SMEM)
ANY = pl.BlockSpec(memory_space=pl.ANY)


def shape(dims, dtype):
    return jax.ShapeDtypeStruct(dims, dtype)


def call(kernel, name, outs, ins, scratch=(), flops=1 << 20, limit=16 * 1024 * 1024, nbytes=1 << 20):
    return pl.pallas_call(
        kernel,
        out_shape=tuple(out for _, out in outs),
        in_specs=[spec for spec, _ in ins],
        out_specs=tuple(spec for spec, _ in outs),
        scratch_shapes=list(scratch),
        name=name,
        compiler_params=pltpu.CompilerParams(vmem_limit_bytes=limit),
        cost_estimate=pl.CostEstimate(flops=flops, bytes_accessed=nbytes, transcendentals=0),
    )(*[array for _, array in ins])


def vmem(arrays):
    return [(VMEM, array) for array in arrays]


def smem(arrays):
    return [(SMEM, array) for array in arrays]


def dot_tn(a, b):
    return lax.dot_general(a, b, (((0,), (0,)), ((), ())), preferred_element_type=F32)


def dot_nn(a, b):
    return lax.dot_general(a, b, (((1,), (0,)), ((), ())), preferred_element_type=F32)


def dot_nt(a, b):
    return lax.dot_general(a, b, (((1,), (1,)), ((), ())), preferred_element_type=F32)


def block_at(number):
    return slice(number * TILE, (number + 1) * TILE)


def fill_slots(part, count, slots, tiles):
    for place in range(count.shape[0]):
        count[place] = 0
    for place in range(slots.shape[0]):
        slots[place] = -1
    for number in range(tiles):
        target = part[number]
        place = count[target]
        count[target] = place + 1
        slots[target * CAP + place] = number


def degree_columns(degrees):
    return jnp.transpose(degrees[...].astype(F32))


def push_kernel(half, src_hbm, part_hbm, dst_hbm, feat_hbm, tiles_hbm, *refs):
    outs = refs[: 2 * half]
    src, part, dst, feat, tiles, product, count, slots, sems = refs[2 * half :]
    copies = [
        pltpu.make_async_copy(source, target, sems.at[number])
        for number, (source, target) in enumerate(
            [
                (part_hbm, part),
                (src_hbm, src),
                (dst_hbm, dst),
                (feat_hbm, feat),
                (tiles_hbm, tiles),
            ]
        )
    ]
    for copy in copies:
        copy.start()
    copies[0].wait()
    fill_slots(part, count, slots, tiles.shape[0])
    for copy in copies[1:]:
        copy.wait()
    for number in range(tiles.shape[0]):
        product[number] = dot_tn(tiles[number], feat[src[number]]).astype(BF16)
    me = lax.axis_index("dom")
    row_at = lax.broadcasted_iota(I32, (TAG_ROWS, product.shape[2]), 0)
    for relative in range(2 * half):
        out = outs[relative]
        target = me ^ relative
        tags = jnp.zeros((TAG_ROWS, product.shape[2]), F32)
        for place in range(CAP):
            number = slots[target * CAP + place]
            held = number >= 0
            tag = jnp.where(held, dst[jnp.maximum(number, 0)] + 1, 0)
            tags = jnp.where(row_at == place, tag.astype(F32), tags)

            @pl.when(held)
            def _():
                out[block_at(place), :] = product[number]

        out[PAIR:, :] = tags.astype(BF16)


def local_kernel(src, dst, feat, tiles, out):
    out[...] = jnp.zeros(out.shape, F32)
    for number in range(tiles.shape[0]):
        out[dst[number]] += dot_tn(tiles[number], feat[src[number]])


def rotate_kernel(first, second, out_first, out_second):
    shards = lax.axis_size("chan")
    me = lax.axis_index("chan")
    width = first.shape[1] // shards
    for own in range(shards):

        @pl.when(me == own)
        def _():
            cut = own * width
            for source, out in ((first, out_first), (second, out_second)):
                out[:, : source.shape[1] - cut] = source[:, cut:]
                if cut:
                    out[:, source.shape[1] - cut :] = source[:, :cut]


def read_tags(pairs, blocks, got):
    channels = pairs[0].shape[1]
    bits = blocks.bit_length()
    per_word = max(1, 24 // (bits * CAP))
    row_at = lax.broadcasted_iota(I32, (TAG_ROWS, channels), 0)
    unit = jnp.zeros((TAG_ROWS, channels), F32)
    for place in range(CAP):
        unit = jnp.where(row_at == place, float(1 << (bits * place)), unit)
    for first in range(0, len(pairs), per_word):
        members = range(first, min(first + per_word, len(pairs)))
        word = jnp.zeros((TAG_ROWS, channels), F32)
        for member in members:
            scale = float(1 << (bits * CAP * (member - first)))
            word = word + pairs[member][PAIR:, :].astype(F32) * (unit * scale)
        packed = jnp.max(jnp.sum(word, axis=0, keepdims=True)).astype(I32)
        for member in members:
            for place in range(CAP):
                shift = bits * (CAP * (member - first) + place)
                got[member * CAP + place] = ((packed >> shift) & (2**bits - 1)) - 1


def add_pairs(pairs, got, acc):
    for number, pair in enumerate(pairs):
        for place in range(CAP):
            block = got[number * CAP + place]

            @pl.when(block >= 0)
            def _():
                acc[block] += pair[block_at(place), :].astype(F32)


def relay_kernel(*refs):
    pairs, (dense, got, acc) = refs[:-3], refs[-3:]
    read_tags(pairs, acc.shape[0], got)
    acc[...] = jnp.zeros(acc.shape, F32)
    add_pairs(pairs, got, acc)
    dense[...] = acc[...].astype(BF16)


def mid_kernel(half, shards, *refs):
    pairs, rest = refs[:half], refs[half:]
    dense, local, feat, w_self, w_neigh, degrees, averaged = rest[:7]
    shares, (got, acc) = rest[7 : 7 + shards], rest[7 + shards :]
    read_tags(pairs, acc.shape[0], got)
    acc[...] = local[...] + dense[...].astype(F32)
    add_pairs(pairs, got, acc)
    divisor = degree_columns(degrees)
    width = shares[0].shape[1]
    for block in range(acc.shape[0]):
        at = block_at(block)
        mean = (acc[block] / divisor[:, block : block + 1]).astype(BF16)
        averaged[at, :] = mean
        value = dot_nn(feat[block], w_self[...]) + dot_nn(mean, w_neigh[...])
        value = value.astype(BF16)
        for piece, share in enumerate(shares):
            share[at, :] = value[:, piece * width : (piece + 1) * width]


def silu_kernel(*refs):
    shares, cotangent, output, slopes = refs[:-3], refs[-3], refs[-2], refs[-1]
    for block in range(output.shape[0] // TILE):
        at = block_at(block)
        value = shares[0][at, :].astype(F32)
        for piece in shares[1:]:
            value = value + piece[at, :].astype(F32)
        gate = 1.0 / (1.0 + jnp.exp(-value))
        output[at, :] = (value * gate).astype(BF16)
        slope = gate * (1.0 + value * (1.0 - gate))
        slopes[at, :] = (cotangent[at, :].astype(F32) * slope).astype(BF16)


def slopes_times(slopes, weights, at):
    width = slopes[0].shape[1]
    total = dot_nt(slopes[0][at, :], weights[:, :width])
    for piece in range(1, len(slopes)):
        columns = slice(piece * width, (piece + 1) * width)
        total = total + dot_nt(slopes[piece][at, :], weights[:, columns])
    return total


def back_kernel(w_neigh, degrees, *refs):
    slopes, back = refs[:-1], refs[-1]
    divisor = degree_columns(degrees)
    for block in range(back.shape[0]):
        total = slopes_times(slopes, w_neigh, block_at(block))
        back[block] = (total / divisor[:, block : block + 1]).astype(BF16)


def spread_kernel(got, rows, *outs):
    for number, out in enumerate(outs, 1):
        for place in range(CAP):
            block = got[number * CAP + place]

            @pl.when(block >= 0)
            def _():
                out[block_at(place), :] = rows[block]


def grads_kernel(inner, feat, averaged, *refs):
    shards = lax.axis_size("chan")
    slopes, outs, whole = refs[:shards], refs[shards:-1], refs[-1]
    channels = feat.shape[1]
    width = slopes[0].shape[1]
    for piece, slope in enumerate(slopes):
        columns = slice(piece * width, (piece + 1) * width)
        whole[:channels, columns] = dot_tn(feat[...], slope[...])
        whole[channels:, columns] = dot_tn(averaged[...], slope[...])
    me = lax.axis_index("dom") & (inner - 1)
    rows = outs[0].shape[0]
    for relative, out in enumerate(outs):
        for owner in range(inner):

            @pl.when((me ^ relative) == owner)
            def _():
                out[...] = whole[owner * rows : (owner + 1) * rows, :].astype(out.dtype)


def gather_sum_kernel(inner, outer, *refs):
    parts, outs, whole = refs[:inner], refs[inner:-1], refs[-1]
    total = parts[0][...]
    for part in parts[1:]:
        total = total + part[...].astype(F32)
    whole[...] = total
    me = lax.axis_index("dom") // inner
    rows = outs[0].shape[0]
    for relative, out in enumerate(outs):
        for owner in range(outer):

            @pl.when((me ^ relative) == owner)
            def _():
                out[...] = whole[owner * rows : (owner + 1) * rows, :].astype(out.dtype)


def last_sum_kernel(*refs):
    parts, out = refs[:-1], refs[-1]
    total = parts[0][...]
    for part in parts[1:]:
        total = total + part[...].astype(F32)
    out[...] = total.astype(BF16)


def place_kernel(shift, *refs):
    parts, out = refs[:-1], refs[-1]
    me = (lax.axis_index("dom") >> shift) & (len(parts) - 1)
    rows = parts[0].shape[0]
    for relative, part in enumerate(parts):
        for owner in range(len(parts)):

            @pl.when((me ^ relative) == owner)
            def _():
                out[owner * rows : (owner + 1) * rows, :] = part[...]


def finish_grads_kernel(scale, *refs):
    parts, outs, whole = refs[:-3], refs[-3:-1], refs[-1]
    place_kernel(0, *parts, whole)
    shards = lax.axis_size("chan")
    me = lax.axis_index("chan")
    columns = whole.shape[1]
    channels = outs[0].shape[0]
    for own in range(shards):

        @pl.when(me == own)
        def _():
            cut = own * (columns // shards)
            for number, out in enumerate(outs):
                rows = slice(number * channels, (number + 1) * channels)
                out[:, cut:] = whole[rows, : columns - cut].astype(F32) * scale
                if cut:
                    out[:, :cut] = whole[rows, columns - cut :].astype(F32) * scale


def local_back_kernel(src, dst, tiles, back, w_self, *refs):
    slopes, out = refs[:-1], refs[-1]
    for block in range(out.shape[0]):
        out[block] = slopes_times(slopes, w_self, block_at(block))
    for number in range(tiles.shape[0]):
        out[src[number]] += dot_nn(tiles[number], back[dst[number]])


def final_kernel(half, src, part, dst, tiles, back, far, partial, *refs):
    near_rows, far_rows = refs[: half - 1], refs[half - 1 : 2 * half - 2]
    out, count, slots, rows, acc = refs[2 * half - 2 :]
    fill_slots(part, count, slots, tiles.shape[0])
    me = lax.axis_index("dom")
    for relative in range(2 * half):
        target = me ^ relative
        shift = relative % half
        for place in range(CAP):
            number = slots[target * CAP + place]

            @pl.when(number >= 0)
            def _():
                if shift:
                    arrived = (near_rows if relative < half else far_rows)[shift - 1]
                    rows[number] = arrived[block_at(place), :]
                else:
                    held = back if relative < half else far
                    rows[number] = held[dst[number]]

    acc[...] = partial[...]
    for number in range(tiles.shape[0]):
        acc[src[number]] += dot_nn(tiles[number], rows[number])
    out[...] = acc[...].astype(BF16)


def swap(value, relative):
    count = lax.axis_size("dom")
    return lax.ppermute(value, "dom", [(at, at ^ relative) for at in range(count)])


def around(value, shift):
    count = lax.axis_size("chan")
    return lax.ppermute(value, "chan", [(at, (at + shift) % count) for at in range(count)])


def after(values, *others):
    return lax.optimization_barrier((tuple(values), others))[0]


def per_device(
    features,
    w_self,
    w_neigh,
    degrees,
    local_src,
    local_dst,
    local_tiles,
    remote_src,
    remote_part,
    remote_dst,
    remote_tiles,
    cotangent,
):
    domains = lax.axis_size("dom")
    shards = lax.axis_size("chan")
    node_rows, channels = features.shape
    out_width = w_self.shape[1]
    own_width = out_width // shards
    blocks = node_rows // TILE
    n_remote = remote_tiles.shape[0]
    half = domains // 2
    inner = 1 << (domains.bit_length() // 2)
    outer = domains // inner
    feat_blocks = features.reshape(blocks, TILE, channels)
    degree_rows = degrees.reshape(blocks, TILE)
    targets = remote_part[:, 0]
    block_shape = (blocks, TILE, channels)
    pair_shape = shape((PAIR + TAG_ROWS, channels), BF16)
    counts = [pltpu.SMEM((domains,), I32), pltpu.SMEM((domains * CAP,), I32)]

    outgoing = call(
        lambda *refs: push_kernel(half, *refs),
        "push",
        [(VMEM, pair_shape)] * domains,
        [(ANY, a) for a in (remote_src, targets, remote_dst, feat_blocks, remote_tiles)],
        [pltpu.SMEM((n_remote,), I32)] * 3
        + [
            pltpu.VMEM(block_shape, BF16),
            pltpu.VMEM(remote_tiles.shape, BF16),
            pltpu.VMEM((n_remote, TILE, channels), BF16),
        ]
        + counts
        + [pltpu.SemaphoreType.DMA((5,))],
        limit=None,
    )
    near, far = outgoing[:half], outgoing[half:]
    relayed = [far[0]] + [swap(far[k], k) for k in range(1, half)]

    (local,) = call(
        local_kernel,
        "local",
        [(VMEM, shape(block_shape, F32))],
        smem([local_src, local_dst]) + vmem([feat_blocks, local_tiles]),
    )
    own_self, own_neigh = call(
        rotate_kernel,
        "rotate",
        [(VMEM, shape(w_self.shape, BF16))] * 2,
        vmem([w_self, w_neigh]),
    )
    dense, got_far = call(
        relay_kernel,
        "relay",
        [(VMEM, shape(block_shape, BF16)), (SMEM, shape((half * CAP,), I32))],
        vmem(relayed),
        [pltpu.VMEM(block_shape, F32)],
    )
    crossed = swap(dense, half)
    near = after(near, dense)
    direct = [near[0]] + [swap(near[k], k) for k in range(1, half)]

    mids = call(
        lambda *refs: mid_kernel(half, shards, *refs),
        "mid",
        [(VMEM, shape((node_rows, channels), BF16))]
        + [(VMEM, shape((node_rows, own_width), BF16))] * shards
        + [(SMEM, shape((half * CAP,), I32))],
        vmem(direct + [crossed, local, feat_blocks, own_self, own_neigh, degree_rows]),
        [pltpu.VMEM(block_shape, F32)],
    )
    averaged, shares, got_near = mids[0], mids[1 : 1 + shards], mids[-1]
    pieces = [shares[0]] + [around(shares[k], k) for k in range(1, shards)]
    output, slopes_own = call(
        silu_kernel,
        "silu",
        [(VMEM, shape((node_rows, own_width), BF16))] * 2,
        vmem(pieces + [cotangent]),
    )
    slopes = [slopes_own] + [around(slopes_own, shards - k) for k in range(1, shards)]

    (back,) = call(
        back_kernel,
        "back",
        [(VMEM, shape(block_shape, BF16))],
        vmem([own_neigh, degree_rows] + slopes),
    )
    back_far = swap(back, half)
    returning = shape((PAIR, channels), BF16)
    near_out = call(
        spread_kernel,
        "spread_near",
        [(VMEM, returning)] * (half - 1),
        [(SMEM, got_near), (VMEM, back)],
    )
    near_back = [swap(rows, k) for k, rows in enumerate(near_out, 1)]

    rows_inner = 2 * channels // inner
    rows_outer = rows_inner // outer
    terms = call(
        lambda *refs: grads_kernel(inner, *refs),
        "grads",
        [(VMEM, shape((rows_inner, out_width), F32))]
        + [(VMEM, shape((rows_inner, out_width), BF16))] * (inner - 1),
        vmem([features, averaged] + slopes),
        [pltpu.VMEM((2 * channels, out_width), F32)],
    )
    terms = [terms[0]] + [swap(terms[k], k) for k in range(1, inner)]
    terms = call(
        lambda *refs: gather_sum_kernel(inner, outer, *refs),
        "grads_inner",
        [(VMEM, shape((rows_outer, out_width), F32))]
        + [(VMEM, shape((rows_outer, out_width), BF16))] * (outer - 1),
        vmem(terms),
        [pltpu.VMEM((rows_inner, out_width), F32)],
    )
    terms = [terms[0]] + [swap(terms[k], k * inner) for k in range(1, outer)]
    (total,) = call(
        last_sum_kernel,
        "grads_outer",
        [(VMEM, shape((rows_outer, out_width), BF16))],
        vmem(terms),
    )
    totals = [total] + [swap(total, k * inner) for k in range(1, outer)]
    (total,) = call(
        lambda *refs: place_kernel(inner.bit_length() - 1, *refs),
        "grads_place",
        [(VMEM, shape((rows_inner, out_width), BF16))],
        vmem(totals),
    )
    totals = [total] + [swap(total, k) for k in range(1, inner)]
    scale = 1.0 / math.sqrt(float(node_rows * domains))
    grad_self, grad_neigh = call(
        lambda *refs: finish_grads_kernel(scale, *refs),
        "grads_finish",
        [(VMEM, shape((channels, out_width), F32))] * 2,
        vmem(totals),
        [pltpu.VMEM((2 * channels, out_width), BF16)],
    )

    far_out = call(
        spread_kernel,
        "spread_far",
        [(VMEM, returning)] * (half - 1),
        [(SMEM, got_far), (VMEM, back_far)],
    )
    far_back = [swap(rows, k) for k, rows in enumerate(far_out, 1)]
    (partial,) = call(
        local_back_kernel,
        "local_back",
        [(VMEM, shape(block_shape, F32))],
        smem([local_src, local_dst]) + vmem([local_tiles, back, own_self] + slopes),
    )
    (grad_features,) = call(
        lambda *refs: final_kernel(half, *refs),
        "final",
        [(VMEM, shape(block_shape, BF16))],
        smem([remote_src, targets, remote_dst])
        + vmem([remote_tiles, back, back_far, partial] + near_back + far_back),
        counts
        + [pltpu.VMEM((n_remote, TILE, channels), BF16), pltpu.VMEM(block_shape, F32)],
    )
    return (output, grad_self, grad_neigh, grad_features.reshape(node_rows, channels))


def solution(mesh):
    in_specs = (
        P("dom", "chan"),
        P("chan", None),
        P("chan", None),
        P("dom"),
        P("dom"),
        P("dom"),
        P("dom", None, None),
        P("dom"),
        P("dom", None),
        P("dom"),
        P("dom", None, None),
        P("dom", "chan"),
    )
    out_specs = (P("dom", "chan"), P("chan", None), P("chan", None), P("dom", "chan"))
    return jax.shard_map(
        per_device, mesh=mesh, in_specs=in_specs, out_specs=out_specs, check_vma=False
    )
```

```python
import math

import jax
import jax.numpy as jnp
from jax import lax
from jax.experimental import pallas as pl
from jax.experimental.pallas import tpu as pltpu
from jax.sharding import PartitionSpec as P


TILE = 128
CAP = 2
TAG_ROWS = 8
PAIR = CAP * TILE

F32 = jnp.float32
BF16 = jnp.bfloat16
I32 = jnp.int32
VMEM = pl.BlockSpec(memory_space=pltpu.VMEM)
SMEM = pl.BlockSpec(memory_space=pltpu.SMEM)
HBM = pl.BlockSpec(memory_space=pltpu.HBM)


def shape(dims, dtype):
    return jax.ShapeDtypeStruct(dims, dtype)


def call(kernel, outs, ins, scratch=(), flops=1 << 20, limit=16 * 1024 * 1024, nbytes=1 << 20):
    return pl.pallas_call(
        kernel,
        out_shape=tuple(out for _, out in outs),
        in_specs=[spec for spec, _ in ins],
        out_specs=tuple(spec for spec, _ in outs),
        scratch_shapes=list(scratch),
        compiler_params=pltpu.CompilerParams(vmem_limit_bytes=limit),
        cost_estimate=pl.CostEstimate(flops=flops, bytes_accessed=nbytes, transcendentals=0),
    )(*[array for _, array in ins])


def vmem(arrays):
    return [(VMEM, array) for array in arrays]


def smem(arrays):
    return [(SMEM, array) for array in arrays]


def dot_tn(a, b):
    return lax.dot_general(a, b, (((0,), (0,)), ((), ())), preferred_element_type=F32)


def dot_nn(a, b):
    return lax.dot_general(a, b, (((1,), (0,)), ((), ())), preferred_element_type=F32)


def dot_nt(a, b):
    return lax.dot_general(a, b, (((1,), (1,)), ((), ())), preferred_element_type=F32)


def block_at(number):
    return slice(number * TILE, (number + 1) * TILE)


def fill_slots(part, count, slots, tiles):
    for place in range(count.shape[0]):
        count[place] = 0
    for place in range(slots.shape[0]):
        slots[place] = -1
    for number in range(tiles):
        target = part[number]
        place = count[target]
        count[target] = place + 1
        slots[target * CAP + place] = number


def degree_columns(degrees):
    return jnp.transpose(degrees[...].astype(F32))


def place_tiles(outs, first, product, slots, tags):
    me = lax.axis_index("dom")
    row_at = lax.broadcasted_iota(I32, (TAG_ROWS, product.shape[2]), 0)
    for relative, out in enumerate(outs, first):
        target = me ^ relative
        marks = jnp.zeros((TAG_ROWS, product.shape[2]), F32)
        for place in range(CAP):
            number = slots[target * CAP + place]
            marks = jnp.where(row_at == place, tags[target * CAP + place].astype(F32), marks)

            @pl.when(number >= 0)
            def _():
                out[block_at(place), :] = product[number]

        out[PAIR:, :] = marks.astype(BF16)


def push_far_kernel(half, src_hbm, part_hbm, dst_hbm, feat_hbm, tiles_hbm, *refs):
    outs, (product, slots, tags) = refs[:half], refs[half : half + 3]
    src, part, dst, feat, tiles, count, sems = refs[half + 3 :]
    pairs = [
        (part_hbm, part),
        (dst_hbm, dst),
        (src_hbm, src),
        (feat_hbm, feat),
        (tiles_hbm, tiles),
    ]
    copies = [
        pltpu.make_async_copy(source, target, sems.at[number])
        for number, (source, target) in enumerate(pairs)
    ]
    for copy in copies:
        copy.start()
    copies[0].wait()
    copies[1].wait()
    fill_slots(part, count, slots, tiles.shape[0])
    for place in range(slots.shape[0]):
        number = slots[place]
        tags[place] = jnp.where(number >= 0, dst[jnp.maximum(number, 0)] + 1, 0)
    for copy in copies[2:]:
        copy.wait()
    for number in range(tiles.shape[0]):
        product[number] = dot_tn(tiles[number], feat[src[number]]).astype(BF16)
    place_tiles(outs, half, product, slots, tags)


def push_near_kernel(product, slots, tags, *outs):
    place_tiles(outs, 0, product, slots, tags)


def local_kernel(src, dst, feat, tiles, out):
    out[...] = jnp.zeros(out.shape, F32)
    for number in range(tiles.shape[0]):
        out[dst[number]] += dot_tn(tiles[number], feat[src[number]])


def rotate_kernel(first, second, out_first, out_second):
    shards = lax.axis_size("chan")
    me = lax.axis_index("chan")
    width = first.shape[1] // shards
    for own in range(shards):

        @pl.when(me == own)
        def _():
            cut = own * width
            for source, out in ((first, out_first), (second, out_second)):
                out[:, : source.shape[1] - cut] = source[:, cut:]
                if cut:
                    out[:, source.shape[1] - cut :] = source[:, :cut]


def read_tags(pairs, blocks, got):
    channels = pairs[0].shape[1]
    bits = blocks.bit_length()
    per_word = max(1, 24 // (bits * CAP))
    row_at = lax.broadcasted_iota(I32, (TAG_ROWS, channels), 0)
    unit = jnp.zeros((TAG_ROWS, channels), F32)
    for place in range(CAP):
        unit = jnp.where(row_at == place, float(1 << (bits * place)), unit)
    for first in range(0, len(pairs), per_word):
        members = range(first, min(first + per_word, len(pairs)))
        word = jnp.zeros((TAG_ROWS, channels), F32)
        for member in members:
            scale = float(1 << (bits * CAP * (member - first)))
            word = word + pairs[member][PAIR:, :].astype(F32) * (unit * scale)
        packed = jnp.max(jnp.sum(word, axis=0, keepdims=True)).astype(I32)
        for member in members:
            for place in range(CAP):
                shift = bits * (CAP * (member - first) + place)
                got[member * CAP + place] = ((packed >> shift) & (2**bits - 1)) - 1


def add_pairs(pairs, got, acc):
    for number, pair in enumerate(pairs):
        for place in range(CAP):
            block = got[number * CAP + place]

            @pl.when(block >= 0)
            def _():
                acc[block] += pair[block_at(place), :].astype(F32)


def relay_kernel(*refs):
    pairs, (dense, got, acc) = refs[:-3], refs[-3:]
    read_tags(pairs, acc.shape[0], got)
    acc[...] = jnp.zeros(acc.shape, F32)
    add_pairs(pairs, got, acc)
    dense[...] = acc[...].astype(BF16)


def mid_kernel(half, shards, *refs):
    pairs, rest = refs[:half], refs[half:]
    dense, local, feat, w_self, w_neigh, degrees, averaged = rest[:7]
    shares, (got, acc) = rest[7 : 7 + shards], rest[7 + shards :]
    read_tags(pairs, acc.shape[0], got)
    acc[...] = local[...] + dense[...].astype(F32)
    add_pairs(pairs, got, acc)
    divisor = degree_columns(degrees)
    width = shares[0].shape[1]
    for block in range(acc.shape[0]):
        at = block_at(block)
        mean = (acc[block] / divisor[:, block : block + 1]).astype(BF16)
        averaged[at, :] = mean
        value = dot_nn(feat[block], w_self[...]) + dot_nn(mean, w_neigh[...])
        value = value.astype(BF16)
        for piece, share in enumerate(shares):
            share[at, :] = value[:, piece * width : (piece + 1) * width]


def silu_kernel(*refs):
    shares, cotangent, output, slopes = refs[:-3], refs[-3], refs[-2], refs[-1]
    for block in range(output.shape[0] // TILE):
        at = block_at(block)
        value = shares[0][at, :].astype(F32)
        for piece in shares[1:]:
            value = value + piece[at, :].astype(F32)
        gate = 1.0 / (1.0 + jnp.exp(-value))
        output[at, :] = (value * gate).astype(BF16)
        slope = gate * (1.0 + value * (1.0 - gate))
        slopes[at, :] = (cotangent[at, :].astype(F32) * slope).astype(BF16)


def slopes_times(slopes, weights, at):
    width = slopes[0].shape[1]
    total = dot_nt(slopes[0][at, :], weights[:, :width])
    for piece in range(1, len(slopes)):
        columns = slice(piece * width, (piece + 1) * width)
        total = total + dot_nt(slopes[piece][at, :], weights[:, columns])
    return total


def back_kernel(w_neigh, degrees, *refs):
    slopes, back = refs[:-1], refs[-1]
    divisor = degree_columns(degrees)
    for block in range(back.shape[0]):
        total = slopes_times(slopes, w_neigh, block_at(block))
        back[block] = (total / divisor[:, block : block + 1]).astype(BF16)


def spread_kernel(got, rows, *outs):
    for number, out in enumerate(outs, 1):
        for place in range(CAP):
            block = got[number * CAP + place]

            @pl.when(block >= 0)
            def _():
                out[block_at(place), :] = rows[block]


def grads_kernel(inner, feat, averaged, *refs):
    shards = lax.axis_size("chan")
    slopes, outs, whole = refs[:shards], refs[shards:-1], refs[-1]
    channels = feat.shape[1]
    width = slopes[0].shape[1]
    for piece, slope in enumerate(slopes):
        columns = slice(piece * width, (piece + 1) * width)
        whole[:channels, columns] = dot_tn(feat[...], slope[...])
        whole[channels:, columns] = dot_tn(averaged[...], slope[...])
    me = lax.axis_index("dom") & (inner - 1)
    rows = outs[0].shape[0]
    for relative, out in enumerate(outs):
        for owner in range(inner):

            @pl.when((me ^ relative) == owner)
            def _():
                out[...] = whole[owner * rows : (owner + 1) * rows, :].astype(out.dtype)


def gather_sum_kernel(*refs):
    parts, out = refs[:-1], refs[-1]
    total = parts[0][...].astype(F32)
    for part in parts[1:]:
        total = total + part[...].astype(F32)
    out[...] = total.astype(BF16)


def place_rows(parts, out):
    me = lax.axis_index("dom") & (len(parts) - 1)
    rows = parts[0].shape[0]
    for relative, part in enumerate(parts):
        for owner in range(len(parts)):

            @pl.when((me ^ relative) == owner)
            def _():
                out[owner * rows : (owner + 1) * rows, :] = part[...]


def finish_grads_kernel(scale, *refs):
    parts, outs, whole = refs[:-3], refs[-3:-1], refs[-1]
    place_rows(parts, whole)
    shards = lax.axis_size("chan")
    me = lax.axis_index("chan")
    columns = whole.shape[1]
    channels = outs[0].shape[0]
    for own in range(shards):

        @pl.when(me == own)
        def _():
            cut = own * (columns // shards)
            for number, out in enumerate(outs):
                rows = slice(number * channels, (number + 1) * channels)
                out[:, cut:] = whole[rows, : columns - cut].astype(F32) * scale
                if cut:
                    out[:, :cut] = whole[rows, columns - cut :].astype(F32) * scale


def local_back_kernel(src, dst, tiles, back, w_self, *refs):
    slopes, out = refs[:-1], refs[-1]
    for block in range(out.shape[0]):
        out[block] = slopes_times(slopes, w_self, block_at(block))
    for number in range(tiles.shape[0]):
        out[src[number]] += dot_nn(tiles[number], back[dst[number]])


def final_kernel(half, src, dst, slots, tiles, back, far, partial, *refs):
    near_rows, far_rows = refs[: half - 1], refs[half - 1 : 2 * half - 2]
    out, rows, acc = refs[2 * half - 2 :]
    me = lax.axis_index("dom")
    for relative in range(2 * half):
        target = me ^ relative
        shift = relative % half
        for place in range(CAP):
            number = slots[target * CAP + place]

            @pl.when(number >= 0)
            def _():
                if shift:
                    arrived = (near_rows if relative < half else far_rows)[shift - 1]
                    rows[number] = arrived[block_at(place), :]
                else:
                    held = back if relative < half else far
                    rows[number] = held[dst[number]]

    acc[...] = partial[...]
    for number in range(tiles.shape[0]):
        acc[src[number]] += dot_nn(tiles[number], rows[number])
    out[...] = acc[...].astype(BF16)


def swap(value, relative):
    count = lax.axis_size("dom")
    pairs = [(at, at ^ relative) for at in range(count)]
    return lax.ppermute(value, "dom", pairs)


def swap_all(values, first):
    out = [values[0]] + [None] * (len(values) - 1)
    for k in range(len(values) - 1, 0, -1):
        out[k] = swap(values[k], k * first)
    return out


def around(value, shift):
    count = lax.axis_size("chan")
    return lax.ppermute(value, "chan", [(at, (at + shift) % count) for at in range(count)])


def per_device(
    features,
    w_self,
    w_neigh,
    degrees,
    local_src,
    local_dst,
    local_tiles,
    remote_src,
    remote_part,
    remote_dst,
    remote_tiles,
    cotangent,
):
    domains = lax.axis_size("dom")
    shards = lax.axis_size("chan")
    node_rows, channels = features.shape
    out_width = w_self.shape[1]
    own_width = out_width // shards
    blocks = node_rows // TILE
    n_remote = remote_tiles.shape[0]
    half = domains // 2
    early = max(1, half // 2)
    inner, outer_bits = inner_and_outer(domains)
    feat_blocks = features.reshape(blocks, TILE, channels)
    degree_rows = degrees.reshape(blocks, TILE)
    targets = remote_part[:, 0]
    block_shape = (blocks, TILE, channels)
    product_shape = (n_remote, TILE, channels)
    pair_shape = shape((PAIR + TAG_ROWS, channels), BF16)
    slot_shape = shape((domains * CAP,), I32)
    got_shape = shape((half * CAP,), I32)

    pushed = call(
        lambda *refs: push_far_kernel(half, *refs),
        [(VMEM, pair_shape)] * half
        + [(VMEM, shape(product_shape, BF16)), (SMEM, slot_shape), (SMEM, slot_shape)],
        [(HBM, a) for a in (remote_src, targets, remote_dst, feat_blocks, remote_tiles)],
        [pltpu.SMEM((n_remote,), I32)] * 3
        + [
            pltpu.VMEM(block_shape, BF16),
            pltpu.VMEM(remote_tiles.shape, BF16),
            pltpu.SMEM((domains,), I32),
            pltpu.SemaphoreType.DMA((5,)),
        ],
        limit=None,
    )
    far, (product, slots, tags) = pushed[:half], pushed[half:]
    relayed = swap_all(far, 1)
    near = call(
        push_near_kernel, [(VMEM, pair_shape)] * half, vmem([product]) + smem([slots, tags])
    )
    near_early = swap_all(near[:early], 1)

    (local,) = call(
        local_kernel,
        [(VMEM, shape(block_shape, F32))],
        smem([local_src, local_dst]) + vmem([feat_blocks, local_tiles]),
    )
    own_self, own_neigh = call(
        rotate_kernel, [(VMEM, shape(w_self.shape, BF16))] * 2, vmem([w_self, w_neigh])
    )
    dense, got_far = call(
        relay_kernel,
        [(VMEM, shape(block_shape, BF16)), (SMEM, got_shape)],
        vmem(relayed),
        [pltpu.VMEM(block_shape, F32)],
    )
    crossed = swap(dense, half)
    near_late = [None] * (half - early)
    for k in range(half - 1, early - 1, -1):
        near_late[k - early] = swap(near[k], k)
    direct = near_early + near_late

    mids = call(
        lambda *refs: mid_kernel(half, shards, *refs),
        [(VMEM, shape((node_rows, channels), BF16))]
        + [(VMEM, shape((node_rows, own_width), BF16))] * shards
        + [(SMEM, got_shape)],
        vmem(direct + [crossed, local, feat_blocks, own_self, own_neigh, degree_rows]),
        [pltpu.VMEM(block_shape, F32)],
    )
    averaged, shares, got_near = mids[0], mids[1 : 1 + shards], mids[-1]
    pieces = [shares[0]] + [around(shares[k], k) for k in range(1, shards)]
    output, slopes_own = call(
        silu_kernel, [(VMEM, shape((node_rows, own_width), BF16))] * 2, vmem(pieces + [cotangent])
    )
    slopes = [slopes_own] + [around(slopes_own, shards - k) for k in range(1, shards)]

    (back,) = call(
        back_kernel, [(VMEM, shape(block_shape, BF16))], vmem([own_neigh, degree_rows] + slopes)
    )
    back_far = swap(back, half)
    returning = shape((PAIR, channels), BF16)
    near_out = call(
        spread_kernel, [(VMEM, returning)] * (half - 1), [(SMEM, got_near), (VMEM, back)]
    )
    near_back = swap_all([None, *near_out], 1)[1:]

    rows_inner = 2 * channels // inner
    terms = call(
        lambda *refs: grads_kernel(inner, *refs),
        [(VMEM, shape((rows_inner, out_width), F32))]
        + [(VMEM, shape((rows_inner, out_width), BF16))] * (inner - 1),
        vmem([features, averaged] + slopes),
        [pltpu.VMEM((2 * channels, out_width), F32)],
    )
    part_shape = shape((rows_inner, out_width), BF16)
    (total,) = call(gather_sum_kernel, [(VMEM, part_shape)], vmem(swap_all(terms, 1)))
    for bit in range(outer_bits):
        arrived = swap(total, inner << bit)
        (total,) = call(gather_sum_kernel, [(VMEM, part_shape)], vmem([total, arrived]))
    totals = swap_all([total] * inner, 1)
    scale = 1.0 / math.sqrt(float(node_rows * domains))
    grad_self, grad_neigh = call(
        lambda *refs: finish_grads_kernel(scale, *refs),
        [(VMEM, shape((channels, out_width), F32))] * 2,
        vmem(totals),
        [pltpu.VMEM((2 * channels, out_width), BF16)],
    )

    far_out = call(
        spread_kernel, [(VMEM, returning)] * (half - 1), [(SMEM, got_far), (VMEM, back_far)]
    )
    far_back = swap_all([None, *far_out], 1)[1:]
    (partial,) = call(
        local_back_kernel,
        [(VMEM, shape(block_shape, F32))],
        smem([local_src, local_dst]) + vmem([local_tiles, back, own_self] + slopes),
    )
    (grad_features,) = call(
        lambda *refs: final_kernel(half, *refs),
        [(VMEM, shape(block_shape, BF16))],
        smem([remote_src, remote_dst, slots])
        + vmem([remote_tiles, back, back_far, partial] + near_back + far_back),
        [pltpu.VMEM(product_shape, BF16), pltpu.VMEM(block_shape, F32)],
    )
    return (output, grad_self, grad_neigh, grad_features.reshape(node_rows, channels))


def inner_and_outer(domains):
    inner_bits = domains.bit_length() // 2
    return 1 << inner_bits, domains.bit_length() - 1 - inner_bits


def solution(mesh):
    in_specs = (
        P("dom", "chan"),
        P("chan", None),
        P("chan", None),
        P("dom"),
        P("dom"),
        P("dom"),
        P("dom", None, None),
        P("dom"),
        P("dom", None),
        P("dom"),
        P("dom", None, None),
        P("dom", "chan"),
    )
    out_specs = (P("dom", "chan"), P("chan", None), P("chan", None), P("dom", "chan"))
    return jax.shard_map(
        per_device, mesh=mesh, in_specs=in_specs, out_specs=out_specs, check_vma=False
    )
```

```python
import math

import jax
import jax.numpy as jnp
from jax import lax
from jax.experimental import pallas as pl
from jax.experimental.pallas import tpu as pltpu
from jax.sharding import PartitionSpec as P


TILE = 128
CAP = 2
TAG_ROWS = 8
PAIR = CAP * TILE

F32 = jnp.float32
BF16 = jnp.bfloat16
I32 = jnp.int32
VMEM = pl.BlockSpec(memory_space=pltpu.VMEM)
SMEM = pl.BlockSpec(memory_space=pltpu.SMEM)
HBM = pl.BlockSpec(memory_space=pltpu.HBM)


def shape(dims, dtype):
    return jax.ShapeDtypeStruct(dims, dtype)


def call(kernel, outs, ins, scratch=(), flops=1 << 20, limit=16 * 1024 * 1024, nbytes=1 << 20):
    return pl.pallas_call(
        kernel,
        out_shape=tuple(out for _, out in outs),
        in_specs=[spec for spec, _ in ins],
        out_specs=tuple(spec for spec, _ in outs),
        scratch_shapes=list(scratch),
        compiler_params=pltpu.CompilerParams(vmem_limit_bytes=limit),
        cost_estimate=pl.CostEstimate(flops=flops, bytes_accessed=nbytes, transcendentals=0),
    )(*[array for _, array in ins])


def vmem(arrays):
    return [(VMEM, array) for array in arrays]


def smem(arrays):
    return [(SMEM, array) for array in arrays]


def dot_tn(a, b):
    return lax.dot_general(a, b, (((0,), (0,)), ((), ())), preferred_element_type=F32)


def dot_nn(a, b):
    return lax.dot_general(a, b, (((1,), (0,)), ((), ())), preferred_element_type=F32)


def dot_nt(a, b):
    return lax.dot_general(a, b, (((1,), (1,)), ((), ())), preferred_element_type=F32)


def block_at(number):
    return slice(number * TILE, (number + 1) * TILE)


def fill_slots(part, count, slots, tiles):
    for place in range(count.shape[0]):
        count[place] = 0
    for place in range(slots.shape[0]):
        slots[place] = -1
    for number in range(tiles):
        target = part[number]
        place = count[target]
        count[target] = place + 1
        slots[target * CAP + place] = number


def degree_columns(degrees):
    return jnp.transpose(degrees[...].astype(F32))


def place_tiles(outs, first, product, slots, tags):
    me = lax.axis_index("dom")
    row_at = lax.broadcasted_iota(I32, (TAG_ROWS, product.shape[2]), 0)
    for relative, out in enumerate(outs, first):
        target = me ^ relative
        marks = jnp.zeros((TAG_ROWS, product.shape[2]), F32)
        for place in range(CAP):
            number = slots[target * CAP + place]
            marks = jnp.where(row_at == place, tags[target * CAP + place].astype(F32), marks)

            @pl.when(number >= 0)
            def _():
                out[block_at(place), :] = product[number]

        out[PAIR:, :] = marks.astype(BF16)


def push_far_kernel(half, src_hbm, part_hbm, dst_hbm, feat_hbm, tiles_hbm, *refs):
    outs, (product, slots, tags) = refs[:half], refs[half : half + 3]
    src, part, dst, feat, tiles, count, sems = refs[half + 3 :]
    pairs = [
        (part_hbm, part),
        (dst_hbm, dst),
        (src_hbm, src),
        (feat_hbm, feat),
        (tiles_hbm, tiles),
    ]
    copies = [
        pltpu.make_async_copy(source, target, sems.at[number])
        for number, (source, target) in enumerate(pairs)
    ]
    for copy in copies:
        copy.start()
    copies[0].wait()
    copies[1].wait()
    fill_slots(part, count, slots, tiles.shape[0])
    for place in range(slots.shape[0]):
        number = slots[place]
        tags[place] = jnp.where(number >= 0, dst[jnp.maximum(number, 0)] + 1, 0)
    for copy in copies[2:]:
        copy.wait()
    for number in range(tiles.shape[0]):
        product[number] = dot_tn(tiles[number], feat[src[number]]).astype(BF16)
    place_tiles(outs, half, product, slots, tags)


def push_near_kernel(product, slots, tags, *outs):
    place_tiles(outs, 0, product, slots, tags)


def local_kernel(src, dst, feat, tiles, out):
    out[...] = jnp.zeros(out.shape, F32)
    for number in range(tiles.shape[0]):
        out[dst[number]] += dot_tn(tiles[number], feat[src[number]])


def rotate_kernel(first, second, out_first, out_second):
    shards = lax.axis_size("chan")
    me = lax.axis_index("chan")
    width = first.shape[1] // shards
    for own in range(shards):

        @pl.when(me == own)
        def _():
            cut = own * width
            for source, out in ((first, out_first), (second, out_second)):
                out[:, : source.shape[1] - cut] = source[:, cut:]
                if cut:
                    out[:, source.shape[1] - cut :] = source[:, :cut]


def read_tags(pairs, blocks, got):
    channels = pairs[0].shape[1]
    bits = blocks.bit_length()
    per_word = max(1, 24 // (bits * CAP))
    row_at = lax.broadcasted_iota(I32, (TAG_ROWS, channels), 0)
    unit = jnp.zeros((TAG_ROWS, channels), F32)
    for place in range(CAP):
        unit = jnp.where(row_at == place, float(1 << (bits * place)), unit)
    for first in range(0, len(pairs), per_word):
        members = range(first, min(first + per_word, len(pairs)))
        word = jnp.zeros((TAG_ROWS, channels), F32)
        for member in members:
            scale = float(1 << (bits * CAP * (member - first)))
            word = word + pairs[member][PAIR:, :].astype(F32) * (unit * scale)
        packed = jnp.max(jnp.sum(word, axis=0, keepdims=True)).astype(I32)
        for member in members:
            for place in range(CAP):
                shift = bits * (CAP * (member - first) + place)
                got[member * CAP + place] = ((packed >> shift) & (2**bits - 1)) - 1


def add_pairs(pairs, got, acc):
    for number, pair in enumerate(pairs):
        for place in range(CAP):
            block = got[number * CAP + place]

            @pl.when(block >= 0)
            def _():
                acc[block] += pair[block_at(place), :].astype(F32)


def relay_kernel(*refs):
    pairs, (dense, got, acc) = refs[:-3], refs[-3:]
    read_tags(pairs, acc.shape[0], got)
    acc[...] = jnp.zeros(acc.shape, F32)
    add_pairs(pairs, got, acc)
    dense[...] = acc[...].astype(BF16)


def mid_kernel(half, shards, *refs):
    pairs, rest = refs[:half], refs[half:]
    dense, local, feat, w_self, w_neigh, degrees, averaged = rest[:7]
    shares, (got, acc) = rest[7 : 7 + shards], rest[7 + shards :]
    read_tags(pairs, acc.shape[0], got)
    acc[...] = local[...] + dense[...].astype(F32)
    add_pairs(pairs, got, acc)
    divisor = degree_columns(degrees)
    width = shares[0].shape[1]
    for block in range(acc.shape[0]):
        at = block_at(block)
        mean = (acc[block] / divisor[:, block : block + 1]).astype(BF16)
        averaged[at, :] = mean
        value = dot_nn(feat[block], w_self[...]) + dot_nn(mean, w_neigh[...])
        value = value.astype(BF16)
        for piece, share in enumerate(shares):
            share[at, :] = value[:, piece * width : (piece + 1) * width]


def silu_kernel(*refs):
    shares, cotangent, output, slopes = refs[:-3], refs[-3], refs[-2], refs[-1]
    for block in range(output.shape[0] // TILE):
        at = block_at(block)
        value = shares[0][at, :].astype(F32)
        for piece in shares[1:]:
            value = value + piece[at, :].astype(F32)
        gate = 1.0 / (1.0 + jnp.exp(-value))
        output[at, :] = (value * gate).astype(BF16)
        slope = gate * (1.0 + value * (1.0 - gate))
        slopes[at, :] = (cotangent[at, :].astype(F32) * slope).astype(BF16)


def slopes_times(slopes, weights, at):
    width = slopes[0].shape[1]
    total = dot_nt(slopes[0][at, :], weights[:, :width])
    for piece in range(1, len(slopes)):
        columns = slice(piece * width, (piece + 1) * width)
        total = total + dot_nt(slopes[piece][at, :], weights[:, columns])
    return total


def back_kernel(w_neigh, degrees, *refs):
    slopes, back = refs[:-1], refs[-1]
    divisor = degree_columns(degrees)
    for block in range(back.shape[0]):
        total = slopes_times(slopes, w_neigh, block_at(block))
        back[block] = (total / divisor[:, block : block + 1]).astype(BF16)


def spread_kernel(got, rows, *outs):
    for number, out in enumerate(outs, 1):
        spread_rows(got, rows, number, out)


def spread_rows(got, rows, number, out):
    for place in range(CAP):
        block = got[number * CAP + place]

        @pl.when(block >= 0)
        def _():
            out[block_at(place), :] = rows[block]


def extra_pieces(total, holder):
    rows, width = total.shape
    channels = holder.shape[1]
    for piece in range(width // channels):
        start = PAIR + piece * rows
        yield slice(piece * channels, (piece + 1) * channels), slice(start, start + rows)


def near_terms_kernel(inner, got, back, feat, averaged, *refs):
    shards = lax.axis_size("chan")
    slopes, own, outs, whole = refs[:shards], refs[shards], refs[shards + 1 : -1], refs[-1]
    channels = feat.shape[1]
    width = slopes[0].shape[1]
    for piece, slope in enumerate(slopes):
        columns = slice(piece * width, (piece + 1) * width)
        whole[:channels, columns] = dot_tn(feat[...], slope[...])
        whole[channels:, columns] = dot_tn(averaged[...], slope[...])
    me = lax.axis_index("dom") & (inner - 1)
    rows = own.shape[0]
    for owner in range(inner):
        at = slice(owner * rows, (owner + 1) * rows)

        @pl.when(me == owner)
        def _():
            own[...] = whole[at, :]

        for relative, out in enumerate(outs, 1):

            @pl.when((me ^ relative) == owner)
            def _():
                for columns, places in extra_pieces(own, out):
                    out[places, :] = whole[at, columns].astype(BF16)

    for relative, out in enumerate(outs, 1):
        spread_rows(got, back, relative, out)


def near_outer_kernel(inner, got, back, own, *refs):
    arrived, total, outs = refs[: inner - 1], refs[inner - 1], refs[inner:]
    for columns, places in extra_pieces(total, outs[0]):
        value = own[:, columns]
        for part in arrived:
            value = value + part[places, :].astype(F32)
        value = value.astype(BF16)
        total[:, columns] = value
        outs[0][places, :] = value
    for relative, out in enumerate(outs, inner):
        spread_rows(got, back, relative, out)


def first_outer_kernel(total, holder, out):
    for columns, places in extra_pieces(total, holder):
        value = total[:, columns].astype(F32) + holder[places, :].astype(F32)
        out[:, columns] = value.astype(BF16)


def outer_kernel(total, arrived, out):
    out[...] = (total[...].astype(F32) + arrived[...].astype(F32)).astype(BF16)


def place_rows(parts, out):
    me = lax.axis_index("dom") & (len(parts) - 1)
    rows = parts[0].shape[0]
    for relative, part in enumerate(parts):
        for owner in range(len(parts)):

            @pl.when((me ^ relative) == owner)
            def _():
                out[owner * rows : (owner + 1) * rows, :] = part[...]


def finish_grads_kernel(scale, *refs):
    parts, outs, whole = refs[:-3], refs[-3:-1], refs[-1]
    place_rows(parts, whole)
    shards = lax.axis_size("chan")
    me = lax.axis_index("chan")
    columns = whole.shape[1]
    channels = outs[0].shape[0]
    for own in range(shards):

        @pl.when(me == own)
        def _():
            cut = own * (columns // shards)
            for number, out in enumerate(outs):
                rows = slice(number * channels, (number + 1) * channels)
                out[:, cut:] = whole[rows, : columns - cut].astype(F32) * scale
                if cut:
                    out[:, :cut] = whole[rows, columns - cut :].astype(F32) * scale


def local_back_kernel(src, dst, tiles, back, w_self, *refs):
    slopes, out = refs[:-1], refs[-1]
    for block in range(out.shape[0]):
        out[block] = slopes_times(slopes, w_self, block_at(block))
    for number in range(tiles.shape[0]):
        out[src[number]] += dot_nn(tiles[number], back[dst[number]])


def final_kernel(half, src, dst, slots, tiles, back, far, partial, *refs):
    near_rows, far_rows = refs[: half - 1], refs[half - 1 : 2 * half - 2]
    out, rows, acc = refs[2 * half - 2 :]
    me = lax.axis_index("dom")
    for relative in range(2 * half):
        target = me ^ relative
        shift = relative % half
        for place in range(CAP):
            number = slots[target * CAP + place]

            @pl.when(number >= 0)
            def _():
                if shift:
                    arrived = (near_rows if relative < half else far_rows)[shift - 1]
                    rows[number] = arrived[block_at(place), :]
                else:
                    held = back if relative < half else far
                    rows[number] = held[dst[number]]

    acc[...] = partial[...]
    for number in range(tiles.shape[0]):
        acc[src[number]] += dot_nn(tiles[number], rows[number])
    out[...] = acc[...].astype(BF16)


def swap(value, relative):
    count = lax.axis_size("dom")
    pairs = [(at, at ^ relative) for at in range(count)]
    return lax.ppermute(value, "dom", pairs)


def swap_all(values, first):
    out = [values[0]] + [None] * (len(values) - 1)
    for k in range(len(values) - 1, 0, -1):
        out[k] = swap(values[k], k * first)
    return out


def around(value, shift):
    count = lax.axis_size("chan")
    return lax.ppermute(value, "chan", [(at, (at + shift) % count) for at in range(count)])


def per_device(
    features,
    w_self,
    w_neigh,
    degrees,
    local_src,
    local_dst,
    local_tiles,
    remote_src,
    remote_part,
    remote_dst,
    remote_tiles,
    cotangent,
):
    domains = lax.axis_size("dom")
    shards = lax.axis_size("chan")
    node_rows, channels = features.shape
    out_width = w_self.shape[1]
    own_width = out_width // shards
    blocks = node_rows // TILE
    n_remote = remote_tiles.shape[0]
    half = domains // 2
    early = max(1, half // 2)
    inner, outer_bits = inner_and_outer(domains)
    feat_blocks = features.reshape(blocks, TILE, channels)
    degree_rows = degrees.reshape(blocks, TILE)
    targets = remote_part[:, 0]
    block_shape = (blocks, TILE, channels)
    product_shape = (n_remote, TILE, channels)
    pair_shape = shape((PAIR + TAG_ROWS, channels), BF16)
    slot_shape = shape((domains * CAP,), I32)
    got_shape = shape((half * CAP,), I32)

    pushed = call(
        lambda *refs: push_far_kernel(half, *refs),
        [(VMEM, pair_shape)] * half
        + [(VMEM, shape(product_shape, BF16)), (SMEM, slot_shape), (SMEM, slot_shape)],
        [(HBM, a) for a in (remote_src, targets, remote_dst, feat_blocks, remote_tiles)],
        [pltpu.SMEM((n_remote,), I32)] * 3
        + [
            pltpu.VMEM(block_shape, BF16),
            pltpu.VMEM(remote_tiles.shape, BF16),
            pltpu.SMEM((domains,), I32),
            pltpu.SemaphoreType.DMA((5,)),
        ],
        limit=None,
    )
    far, (product, slots, tags) = pushed[:half], pushed[half:]
    relayed = swap_all(far, 1)
    near = call(
        push_near_kernel, [(VMEM, pair_shape)] * half, vmem([product]) + smem([slots, tags])
    )
    near_early = swap_all(near[:early], 1)

    (local,) = call(
        local_kernel,
        [(VMEM, shape(block_shape, F32))],
        smem([local_src, local_dst]) + vmem([feat_blocks, local_tiles]),
    )
    own_self, own_neigh = call(
        rotate_kernel, [(VMEM, shape(w_self.shape, BF16))] * 2, vmem([w_self, w_neigh])
    )
    dense, got_far = call(
        relay_kernel,
        [(VMEM, shape(block_shape, BF16)), (SMEM, got_shape)],
        vmem(relayed),
        [pltpu.VMEM(block_shape, F32)],
    )
    crossed = swap(dense, half)
    near_late = [None] * (half - early)
    for k in range(half - 1, early - 1, -1):
        near_late[k - early] = swap(near[k], k)
    direct = near_early + near_late

    mids = call(
        lambda *refs: mid_kernel(half, shards, *refs),
        [(VMEM, shape((node_rows, channels), BF16))]
        + [(VMEM, shape((node_rows, own_width), BF16))] * shards
        + [(SMEM, got_shape)],
        vmem(direct + [crossed, local, feat_blocks, own_self, own_neigh, degree_rows]),
        [pltpu.VMEM(block_shape, F32)],
    )
    averaged, shares, got_near = mids[0], mids[1 : 1 + shards], mids[-1]
    pieces = [shares[0]] + [around(shares[k], k) for k in range(1, shards)]
    output, slopes_own = call(
        silu_kernel, [(VMEM, shape((node_rows, own_width), BF16))] * 2, vmem(pieces + [cotangent])
    )
    slopes = [slopes_own] + [around(slopes_own, shards - k) for k in range(1, shards)]

    (back,) = call(
        back_kernel, [(VMEM, shape(block_shape, BF16))], vmem([own_neigh, degree_rows] + slopes)
    )
    back_far = swap(back, half)
    returning = shape((PAIR, channels), BF16)
    rows_inner = 2 * channels // inner
    loaded = shape((PAIR + rows_inner * out_width // channels, channels), BF16)
    part_shape = shape((rows_inner, out_width), BF16)
    own_terms, *near_out = call(
        lambda *refs: near_terms_kernel(inner, *refs),
        [(VMEM, shape((rows_inner, out_width), F32))] + [(VMEM, loaded)] * (inner - 1),
        smem([got_near]) + vmem([back, features, averaged] + slopes),
        [pltpu.VMEM((2 * channels, out_width), F32)],
    )
    near_back = swap_all([None, *near_out], 1)[1:]
    total, *near_out = call(
        lambda *refs: near_outer_kernel(inner, *refs),
        [(VMEM, part_shape), (VMEM, loaded)] + [(VMEM, returning)] * (half - inner - 1),
        smem([got_near]) + vmem([back, own_terms] + near_back),
    )
    outer_back = [None] * (half - inner)
    for k in range(half - 1, inner - 1, -1):
        outer_back[k - inner] = swap(near_out[k - inner], k)
    near_back = near_back + outer_back
    (total,) = call(first_outer_kernel, [(VMEM, part_shape)], vmem([total, outer_back[0]]))
    for bit in range(1, outer_bits):
        arrived = swap(total, inner << bit)
        (total,) = call(outer_kernel, [(VMEM, part_shape)], vmem([total, arrived]))
    totals = swap_all([total] * inner, 1)
    scale = 1.0 / math.sqrt(float(node_rows * domains))
    grad_self, grad_neigh = call(
        lambda *refs: finish_grads_kernel(scale, *refs),
        [(VMEM, shape((channels, out_width), F32))] * 2,
        vmem(totals),
        [pltpu.VMEM((2 * channels, out_width), BF16)],
    )

    far_out = call(
        spread_kernel, [(VMEM, returning)] * (half - 1), [(SMEM, got_far), (VMEM, back_far)]
    )
    far_back = swap_all([None, *far_out], 1)[1:]
    (partial,) = call(
        local_back_kernel,
        [(VMEM, shape(block_shape, F32))],
        smem([local_src, local_dst]) + vmem([local_tiles, back, own_self] + slopes),
    )
    (grad_features,) = call(
        lambda *refs: final_kernel(half, *refs),
        [(VMEM, shape(block_shape, BF16))],
        smem([remote_src, remote_dst, slots])
        + vmem([remote_tiles, back, back_far, partial] + near_back + far_back),
        [pltpu.VMEM(product_shape, BF16), pltpu.VMEM(block_shape, F32)],
    )
    return (output, grad_self, grad_neigh, grad_features.reshape(node_rows, channels))


def inner_and_outer(domains):
    inner_bits = domains.bit_length() // 2
    return 1 << inner_bits, domains.bit_length() - 1 - inner_bits


def solution(mesh):
    in_specs = (
        P("dom", "chan"),
        P("chan", None),
        P("chan", None),
        P("dom"),
        P("dom"),
        P("dom"),
        P("dom", None, None),
        P("dom"),
        P("dom", None),
        P("dom"),
        P("dom", None, None),
        P("dom", "chan"),
    )
    out_specs = (P("dom", "chan"), P("chan", None), P("chan", None), P("dom", "chan"))
    return jax.shard_map(
        per_device, mesh=mesh, in_specs=in_specs, out_specs=out_specs, check_vma=False
    )
```

```python
import math

import jax
import jax.numpy as jnp
from jax import lax
from jax.experimental import pallas as pl
from jax.experimental.pallas import tpu as pltpu
from jax.sharding import PartitionSpec as P


TILE = 128
CAP = 2
TAG_ROWS = 8
PAIR = CAP * TILE

F32 = jnp.float32
BF16 = jnp.bfloat16
I32 = jnp.int32
VMEM = pl.BlockSpec(memory_space=pltpu.VMEM)
SMEM = pl.BlockSpec(memory_space=pltpu.SMEM)
HBM = pl.BlockSpec(memory_space=pltpu.HBM)


def shape(dims, dtype):
    return jax.ShapeDtypeStruct(dims, dtype)


def call(kernel, outs, ins, scratch=(), flops=1 << 20, limit=16 * 1024 * 1024, nbytes=1 << 20):
    return pl.pallas_call(
        kernel,
        out_shape=tuple(out for _, out in outs),
        in_specs=[spec for spec, _ in ins],
        out_specs=tuple(spec for spec, _ in outs),
        scratch_shapes=list(scratch),
        compiler_params=pltpu.CompilerParams(vmem_limit_bytes=limit),
        cost_estimate=pl.CostEstimate(flops=flops, bytes_accessed=nbytes, transcendentals=0),
    )(*[array for _, array in ins])


def vmem(arrays):
    return [(VMEM, array) for array in arrays]


def smem(arrays):
    return [(SMEM, array) for array in arrays]


def dot_tn(a, b):
    return lax.dot_general(a, b, (((0,), (0,)), ((), ())), preferred_element_type=F32)


def dot_nn(a, b):
    return lax.dot_general(a, b, (((1,), (0,)), ((), ())), preferred_element_type=F32)


def dot_nt(a, b):
    return lax.dot_general(a, b, (((1,), (1,)), ((), ())), preferred_element_type=F32)


def block_at(number):
    return slice(number * TILE, (number + 1) * TILE)


def fill_slots(part, count, slots, tiles):
    for place in range(count.shape[0]):
        count[place] = 0
    for place in range(slots.shape[0]):
        slots[place] = -1
    for number in range(tiles):
        target = part[number]
        place = count[target]
        count[target] = place + 1
        slots[target * CAP + place] = number


def degree_columns(degrees):
    return jnp.transpose(degrees[...].astype(F32))


def place_tiles(outs, first, product, slots, tags):
    me = lax.axis_index("dom")
    row_at = lax.broadcasted_iota(I32, (TAG_ROWS, product.shape[2]), 0)
    for relative, out in enumerate(outs, first):
        target = me ^ relative
        marks = jnp.zeros((TAG_ROWS, product.shape[2]), F32)
        for place in range(CAP):
            number = slots[target * CAP + place]
            marks = jnp.where(row_at == place, tags[target * CAP + place].astype(F32), marks)

            @pl.when(number >= 0)
            def _():
                out[block_at(place), :] = product[number]

        out[PAIR:, :] = marks.astype(BF16)


def push_far_kernel(half, src_hbm, part_hbm, dst_hbm, feat_hbm, tiles_hbm, *refs):
    outs, (product, slots, tags) = refs[:half], refs[half : half + 3]
    src, part, dst, feat, tiles, count, sems = refs[half + 3 :]
    pairs = [
        (part_hbm, part),
        (dst_hbm, dst),
        (src_hbm, src),
        (feat_hbm, feat),
        (tiles_hbm, tiles),
    ]
    copies = [
        pltpu.make_async_copy(source, target, sems.at[number])
        for number, (source, target) in enumerate(pairs)
    ]
    for copy in copies:
        copy.start()
    copies[0].wait()
    copies[1].wait()
    fill_slots(part, count, slots, tiles.shape[0])
    for place in range(slots.shape[0]):
        number = slots[place]
        tags[place] = jnp.where(number >= 0, dst[jnp.maximum(number, 0)] + 1, 0)
    for copy in copies[2:]:
        copy.wait()
    for number in range(tiles.shape[0]):
        product[number] = dot_tn(tiles[number], feat[src[number]]).astype(BF16)
    place_tiles(outs, half, product, slots, tags)


def push_near_kernel(product, slots, tags, *outs):
    place_tiles(outs, 0, product, slots, tags)


def local_kernel(src, dst, feat, tiles, out):
    out[...] = jnp.zeros(out.shape, F32)
    for number in range(tiles.shape[0]):
        out[dst[number]] += dot_tn(tiles[number], feat[src[number]])


def rotate_kernel(first, second, out_first, out_second):
    shards = lax.axis_size("chan")
    me = lax.axis_index("chan")
    width = first.shape[1] // shards
    for own in range(shards):

        @pl.when(me == own)
        def _():
            cut = own * width
            for source, out in ((first, out_first), (second, out_second)):
                out[:, : source.shape[1] - cut] = source[:, cut:]
                if cut:
                    out[:, source.shape[1] - cut :] = source[:, :cut]


def read_tags(pairs, blocks, got):
    channels = pairs[0].shape[1]
    bits = blocks.bit_length()
    per_word = max(1, 24 // (bits * CAP))
    row_at = lax.broadcasted_iota(I32, (TAG_ROWS, channels), 0)
    unit = jnp.zeros((TAG_ROWS, channels), F32)
    for place in range(CAP):
        unit = jnp.where(row_at == place, float(1 << (bits * place)), unit)
    for first in range(0, len(pairs), per_word):
        members = range(first, min(first + per_word, len(pairs)))
        word = jnp.zeros((TAG_ROWS, channels), F32)
        for member in members:
            scale = float(1 << (bits * CAP * (member - first)))
            word = word + pairs[member][PAIR:, :].astype(F32) * (unit * scale)
        packed = jnp.max(jnp.sum(word, axis=0, keepdims=True)).astype(I32)
        for member in members:
            for place in range(CAP):
                shift = bits * (CAP * (member - first) + place)
                got[member * CAP + place] = ((packed >> shift) & (2**bits - 1)) - 1


def add_pairs(pairs, got, acc):
    for number, pair in enumerate(pairs):
        for place in range(CAP):
            block = got[number * CAP + place]

            @pl.when(block >= 0)
            def _():
                acc[block] += pair[block_at(place), :].astype(F32)


def relay_kernel(*refs):
    pairs, (dense, got, acc) = refs[:-3], refs[-3:]
    read_tags(pairs, acc.shape[0], got)
    acc[...] = jnp.zeros(acc.shape, F32)
    add_pairs(pairs, got, acc)
    dense[...] = acc[...].astype(BF16)


def mid_kernel(half, shards, *refs):
    pairs, rest = refs[:half], refs[half:]
    dense, local, feat, w_self, w_neigh, degrees, averaged = rest[:7]
    shares, (got, acc) = rest[7 : 7 + shards], rest[7 + shards :]
    read_tags(pairs, acc.shape[0], got)
    acc[...] = local[...] + dense[...].astype(F32)
    add_pairs(pairs, got, acc)
    divisor = degree_columns(degrees)
    width = shares[0].shape[1]
    for block in range(acc.shape[0]):
        at = block_at(block)
        mean = (acc[block] / divisor[:, block : block + 1]).astype(BF16)
        averaged[at, :] = mean
        value = dot_nn(feat[block], w_self[...]) + dot_nn(mean, w_neigh[...])
        value = value.astype(BF16)
        for piece, share in enumerate(shares):
            share[at, :] = value[:, piece * width : (piece + 1) * width]


def silu_kernel(*refs):
    shares, cotangent, output, slopes = refs[:-3], refs[-3], refs[-2], refs[-1]
    for block in range(output.shape[0] // TILE):
        at = block_at(block)
        value = shares[0][at, :].astype(F32)
        for piece in shares[1:]:
            value = value + piece[at, :].astype(F32)
        gate = 1.0 / (1.0 + jnp.exp(-value))
        output[at, :] = (value * gate).astype(BF16)
        slope = gate * (1.0 + value * (1.0 - gate))
        slopes[at, :] = (cotangent[at, :].astype(F32) * slope).astype(BF16)


def slopes_times(slopes, weights, at):
    width = slopes[0].shape[1]
    total = dot_nt(slopes[0][at, :], weights[:, :width])
    for piece in range(1, len(slopes)):
        columns = slice(piece * width, (piece + 1) * width)
        total = total + dot_nt(slopes[piece][at, :], weights[:, columns])
    return total


def back_kernel(w_neigh, degrees, *refs):
    slopes, back = refs[:-1], refs[-1]
    divisor = degree_columns(degrees)
    for block in range(back.shape[0]):
        total = slopes_times(slopes, w_neigh, block_at(block))
        back[block] = (total / divisor[:, block : block + 1]).astype(BF16)


def spread_kernel(got, rows, *outs):
    for number, out in enumerate(outs, 1):
        for place in range(CAP):
            block = got[number * CAP + place]

            @pl.when(block >= 0)
            def _():
                out[block_at(place), :] = rows[block]


def grads_kernel(inner, feat, averaged, *refs):
    shards = lax.axis_size("chan")
    slopes, outs, whole = refs[:shards], refs[shards:-1], refs[-1]
    channels = feat.shape[1]
    width = slopes[0].shape[1]
    for piece, slope in enumerate(slopes):
        columns = slice(piece * width, (piece + 1) * width)
        whole[:channels, columns] = dot_tn(feat[...], slope[...])
        whole[channels:, columns] = dot_tn(averaged[...], slope[...])
    me = lax.axis_index("dom") & (inner - 1)
    rows = outs[0].shape[0]
    for relative, out in enumerate(outs):
        for owner in range(inner):

            @pl.when((me ^ relative) == owner)
            def _():
                out[...] = whole[owner * rows : (owner + 1) * rows, :].astype(out.dtype)


def gather_sum_kernel(*refs):
    parts, out = refs[:-1], refs[-1]
    total = parts[0][...].astype(F32)
    for part in parts[1:]:
        total = total + part[...].astype(F32)
    out[...] = total.astype(BF16)


def place_rows(parts, out):
    me = lax.axis_index("dom") & (len(parts) - 1)
    rows = parts[0].shape[0]
    for relative, part in enumerate(parts):
        for owner in range(len(parts)):

            @pl.when((me ^ relative) == owner)
            def _():
                out[owner * rows : (owner + 1) * rows, :] = part[...]


def finish_grads_kernel(scale, *refs):
    parts, outs, whole = refs[:-3], refs[-3:-1], refs[-1]
    place_rows(parts, whole)
    shards = lax.axis_size("chan")
    me = lax.axis_index("chan")
    columns = whole.shape[1]
    channels = outs[0].shape[0]
    for own in range(shards):

        @pl.when(me == own)
        def _():
            cut = own * (columns // shards)
            for number, out in enumerate(outs):
                rows = slice(number * channels, (number + 1) * channels)
                out[:, cut:] = whole[rows, : columns - cut].astype(F32) * scale
                if cut:
                    out[:, :cut] = whole[rows, columns - cut :].astype(F32) * scale


def local_back_kernel(src, dst, tiles, back, w_self, *refs):
    slopes, out = refs[:-1], refs[-1]
    for block in range(out.shape[0]):
        out[block] = slopes_times(slopes, w_self, block_at(block))
    for number in range(tiles.shape[0]):
        out[src[number]] += dot_nn(tiles[number], back[dst[number]])


def final_kernel(half, src, dst, slots, tiles, back, far, partial, *refs):
    near_rows, far_rows = refs[: half - 1], refs[half - 1 : 2 * half - 2]
    out, rows, acc = refs[2 * half - 2 :]
    me = lax.axis_index("dom")
    for relative in range(2 * half):
        target = me ^ relative
        shift = relative % half
        for place in range(CAP):
            number = slots[target * CAP + place]

            @pl.when(number >= 0)
            def _():
                if shift:
                    arrived = (near_rows if relative < half else far_rows)[shift - 1]
                    rows[number] = arrived[block_at(place), :]
                else:
                    held = back if relative < half else far
                    rows[number] = held[dst[number]]

    acc[...] = partial[...]
    for number in range(tiles.shape[0]):
        acc[src[number]] += dot_nn(tiles[number], rows[number])
    out[...] = acc[...].astype(BF16)


def swap(value, relative):
    count = lax.axis_size("dom")
    pairs = [(at, at ^ relative) for at in range(count)]
    return lax.ppermute(value, "dom", pairs)


def nearest_first(top, bottom=1):
    return sorted(range(bottom, top), key=lambda k: (k.bit_count(), -k))


def swap_all(values, first):
    out = [values[0]] + [None] * (len(values) - 1)
    for k in nearest_first(len(values)):
        out[k] = swap(values[k], k * first)
    return out


def around(value, shift):
    count = lax.axis_size("chan")
    return lax.ppermute(value, "chan", [(at, (at + shift) % count) for at in range(count)])


def per_device(
    features,
    w_self,
    w_neigh,
    degrees,
    local_src,
    local_dst,
    local_tiles,
    remote_src,
    remote_part,
    remote_dst,
    remote_tiles,
    cotangent,
):
    domains = lax.axis_size("dom")
    shards = lax.axis_size("chan")
    node_rows, channels = features.shape
    out_width = w_self.shape[1]
    own_width = out_width // shards
    blocks = node_rows // TILE
    n_remote = remote_tiles.shape[0]
    half = domains // 2
    early = max(1, half // 2)
    inner, outer_bits = inner_and_outer(domains)
    feat_blocks = features.reshape(blocks, TILE, channels)
    degree_rows = degrees.reshape(blocks, TILE)
    targets = remote_part[:, 0]
    block_shape = (blocks, TILE, channels)
    product_shape = (n_remote, TILE, channels)
    pair_shape = shape((PAIR + TAG_ROWS, channels), BF16)
    slot_shape = shape((domains * CAP,), I32)
    got_shape = shape((half * CAP,), I32)

    pushed = call(
        lambda *refs: push_far_kernel(half, *refs),
        [(VMEM, pair_shape)] * half
        + [(VMEM, shape(product_shape, BF16)), (SMEM, slot_shape), (SMEM, slot_shape)],
        [(HBM, a) for a in (remote_src, targets, remote_dst, feat_blocks, remote_tiles)],
        [pltpu.SMEM((n_remote,), I32)] * 3
        + [
            pltpu.VMEM(block_shape, BF16),
            pltpu.VMEM(remote_tiles.shape, BF16),
            pltpu.SMEM((domains,), I32),
            pltpu.SemaphoreType.DMA((5,)),
        ],
        limit=None,
    )
    far, (product, slots, tags) = pushed[:half], pushed[half:]
    relayed = swap_all(far, 1)
    near = call(
        push_near_kernel, [(VMEM, pair_shape)] * half, vmem([product]) + smem([slots, tags])
    )
    near_early = swap_all(near[:early], 1)

    (local,) = call(
        local_kernel,
        [(VMEM, shape(block_shape, F32))],
        smem([local_src, local_dst]) + vmem([feat_blocks, local_tiles]),
    )
    own_self, own_neigh = call(
        rotate_kernel, [(VMEM, shape(w_self.shape, BF16))] * 2, vmem([w_self, w_neigh])
    )
    dense, got_far = call(
        relay_kernel,
        [(VMEM, shape(block_shape, BF16)), (SMEM, got_shape)],
        vmem(relayed),
        [pltpu.VMEM(block_shape, F32)],
    )
    crossed = swap(dense, half)
    near_late = [None] * (half - early)
    for k in nearest_first(half, early):
        near_late[k - early] = swap(near[k], k)
    direct = near_early + near_late

    mids = call(
        lambda *refs: mid_kernel(half, shards, *refs),
        [(VMEM, shape((node_rows, channels), BF16))]
        + [(VMEM, shape((node_rows, own_width), BF16))] * shards
        + [(SMEM, got_shape)],
        vmem(direct + [crossed, local, feat_blocks, own_self, own_neigh, degree_rows]),
        [pltpu.VMEM(block_shape, F32)],
    )
    averaged, shares, got_near = mids[0], mids[1 : 1 + shards], mids[-1]
    pieces = [shares[0]] + [around(shares[k], k) for k in range(1, shards)]
    output, slopes_own = call(
        silu_kernel, [(VMEM, shape((node_rows, own_width), BF16))] * 2, vmem(pieces + [cotangent])
    )
    slopes = [slopes_own] + [around(slopes_own, shards - k) for k in range(1, shards)]

    (back,) = call(
        back_kernel, [(VMEM, shape(block_shape, BF16))], vmem([own_neigh, degree_rows] + slopes)
    )
    back_far = swap(back, half)
    returning = shape((PAIR, channels), BF16)
    near_out = call(
        spread_kernel, [(VMEM, returning)] * (half - 1), [(SMEM, got_near), (VMEM, back)]
    )
    near_back = swap_all([None, *near_out], 1)[1:]

    rows_inner = 2 * channels // inner
    terms = call(
        lambda *refs: grads_kernel(inner, *refs),
        [(VMEM, shape((rows_inner, out_width), F32))]
        + [(VMEM, shape((rows_inner, out_width), BF16))] * (inner - 1),
        vmem([features, averaged] + slopes),
        [pltpu.VMEM((2 * channels, out_width), F32)],
    )
    part_shape = shape((rows_inner, out_width), BF16)
    (total,) = call(gather_sum_kernel, [(VMEM, part_shape)], vmem(swap_all(terms, 1)))
    for bit in range(outer_bits):
        arrived = swap(total, inner << bit)
        (total,) = call(gather_sum_kernel, [(VMEM, part_shape)], vmem([total, arrived]))
    totals = swap_all([total] * inner, 1)
    scale = 1.0 / math.sqrt(float(node_rows * domains))
    grad_self, grad_neigh = call(
        lambda *refs: finish_grads_kernel(scale, *refs),
        [(VMEM, shape((channels, out_width), F32))] * 2,
        vmem(totals),
        [pltpu.VMEM((2 * channels, out_width), BF16)],
    )

    far_out = call(
        spread_kernel, [(VMEM, returning)] * (half - 1), [(SMEM, got_far), (VMEM, back_far)]
    )
    far_back = swap_all([None, *far_out], 1)[1:]
    (partial,) = call(
        local_back_kernel,
        [(VMEM, shape(block_shape, F32))],
        smem([local_src, local_dst]) + vmem([local_tiles, back, own_self] + slopes),
    )
    (grad_features,) = call(
        lambda *refs: final_kernel(half, *refs),
        [(VMEM, shape(block_shape, BF16))],
        smem([remote_src, remote_dst, slots])
        + vmem([remote_tiles, back, back_far, partial] + near_back + far_back),
        [pltpu.VMEM(product_shape, BF16), pltpu.VMEM(block_shape, F32)],
    )
    return (output, grad_self, grad_neigh, grad_features.reshape(node_rows, channels))


def inner_and_outer(domains):
    inner_bits = domains.bit_length() // 2
    return 1 << inner_bits, domains.bit_length() - 1 - inner_bits


def solution(mesh):
    in_specs = (
        P("dom", "chan"),
        P("chan", None),
        P("chan", None),
        P("dom"),
        P("dom"),
        P("dom"),
        P("dom", None, None),
        P("dom"),
        P("dom", None),
        P("dom"),
        P("dom", None, None),
        P("dom", "chan"),
    )
    out_specs = (P("dom", "chan"), P("chan", None), P("chan", None), P("dom", "chan"))
    return jax.shard_map(
        per_device, mesh=mesh, in_specs=in_specs, out_specs=out_specs, check_vma=False
    )
```

```python
import math

import jax
import jax.numpy as jnp
from jax import lax
from jax.experimental import pallas as pl
from jax.experimental.pallas import tpu as pltpu
from jax.sharding import PartitionSpec as P


TILE = 128
CAP = 2
TAG_ROWS = 8
PAIR = CAP * TILE

F32 = jnp.float32
BF16 = jnp.bfloat16
I32 = jnp.int32
VMEM = pl.BlockSpec(memory_space=pltpu.VMEM)
SMEM = pl.BlockSpec(memory_space=pltpu.SMEM)
HBM = pl.BlockSpec(memory_space=pltpu.HBM)


def shape(dims, dtype):
    return jax.ShapeDtypeStruct(dims, dtype)


def call(kernel, outs, ins, scratch=(), flops=1 << 20, limit=16 * 1024 * 1024, nbytes=1 << 20):
    return pl.pallas_call(
        kernel,
        out_shape=tuple(out for _, out in outs),
        in_specs=[spec for spec, _ in ins],
        out_specs=tuple(spec for spec, _ in outs),
        scratch_shapes=list(scratch),
        compiler_params=pltpu.CompilerParams(vmem_limit_bytes=limit),
        cost_estimate=pl.CostEstimate(flops=flops, bytes_accessed=nbytes, transcendentals=0),
    )(*[array for _, array in ins])


def vmem(arrays):
    return [(VMEM, array) for array in arrays]


def smem(arrays):
    return [(SMEM, array) for array in arrays]


def dot_tn(a, b):
    return lax.dot_general(a, b, (((0,), (0,)), ((), ())), preferred_element_type=F32)


def dot_nn(a, b):
    return lax.dot_general(a, b, (((1,), (0,)), ((), ())), preferred_element_type=F32)


def dot_nt(a, b):
    return lax.dot_general(a, b, (((1,), (1,)), ((), ())), preferred_element_type=F32)


def block_at(number):
    return slice(number * TILE, (number + 1) * TILE)


def fill_slots(part, count, slots, tiles):
    for place in range(count.shape[0]):
        count[place] = 0
    for place in range(slots.shape[0]):
        slots[place] = -1
    for number in range(tiles):
        target = part[number]
        place = count[target]
        count[target] = place + 1
        slots[target * CAP + place] = number


def degree_columns(degrees):
    return jnp.transpose(degrees[...].astype(F32))


def place_tiles(outs, first, product, slots, tags):
    me = lax.axis_index("dom")
    row_at = lax.broadcasted_iota(I32, (TAG_ROWS, product.shape[2]), 0)
    for relative, out in enumerate(outs, first):
        target = me ^ relative
        marks = jnp.zeros((TAG_ROWS, product.shape[2]), F32)
        for place in range(CAP):
            number = slots[target * CAP + place]
            marks = jnp.where(row_at == place, tags[target * CAP + place].astype(F32), marks)

            @pl.when(number >= 0)
            def _():
                out[block_at(place), :] = product[number]

        out[PAIR:, :] = marks.astype(BF16)


def push_far_kernel(half, src_hbm, part_hbm, dst_hbm, feat_hbm, tiles_hbm, *refs):
    outs, (product, slots, tags) = refs[:half], refs[half : half + 3]
    src, part, dst, feat, tiles, count, sems = refs[half + 3 :]
    pairs = [
        (part_hbm, part),
        (dst_hbm, dst),
        (src_hbm, src),
        (feat_hbm, feat),
        (tiles_hbm, tiles),
    ]
    copies = [
        pltpu.make_async_copy(source, target, sems.at[number])
        for number, (source, target) in enumerate(pairs)
    ]
    for copy in copies:
        copy.start()
    copies[0].wait()
    copies[1].wait()
    fill_slots(part, count, slots, tiles.shape[0])
    for place in range(slots.shape[0]):
        number = slots[place]
        tags[place] = jnp.where(number >= 0, dst[jnp.maximum(number, 0)] + 1, 0)
    for copy in copies[2:]:
        copy.wait()
    for number in range(tiles.shape[0]):
        product[number] = dot_tn(tiles[number], feat[src[number]]).astype(BF16)
    place_tiles(outs, half, product, slots, tags)


def push_near_kernel(product, slots, tags, *outs):
    place_tiles(outs, 0, product, slots, tags)


def local_kernel(src, dst, feat, tiles, out):
    out[...] = jnp.zeros(out.shape, F32)
    for number in range(tiles.shape[0]):
        out[dst[number]] += dot_tn(tiles[number], feat[src[number]])


def rotate_kernel(first, second, out_first, out_second):
    shards = lax.axis_size("chan")
    me = lax.axis_index("chan")
    width = first.shape[1] // shards
    for own in range(shards):

        @pl.when(me == own)
        def _():
            cut = own * width
            for source, out in ((first, out_first), (second, out_second)):
                out[:, : source.shape[1] - cut] = source[:, cut:]
                if cut:
                    out[:, source.shape[1] - cut :] = source[:, :cut]


def read_tags(pairs, blocks, got):
    channels = pairs[0].shape[1]
    bits = blocks.bit_length()
    per_word = max(1, 24 // (bits * CAP))
    row_at = lax.broadcasted_iota(I32, (TAG_ROWS, channels), 0)
    unit = jnp.zeros((TAG_ROWS, channels), F32)
    for place in range(CAP):
        unit = jnp.where(row_at == place, float(1 << (bits * place)), unit)
    for first in range(0, len(pairs), per_word):
        members = range(first, min(first + per_word, len(pairs)))
        word = jnp.zeros((TAG_ROWS, channels), F32)
        for member in members:
            scale = float(1 << (bits * CAP * (member - first)))
            word = word + pairs[member][PAIR:, :].astype(F32) * (unit * scale)
        packed = jnp.max(jnp.sum(word, axis=0, keepdims=True)).astype(I32)
        for member in members:
            for place in range(CAP):
                shift = bits * (CAP * (member - first) + place)
                got[member * CAP + place] = ((packed >> shift) & (2**bits - 1)) - 1


def add_pairs(pairs, got, acc):
    for number, pair in enumerate(pairs):
        for place in range(CAP):
            block = got[number * CAP + place]

            @pl.when(block >= 0)
            def _():
                acc[block] += pair[block_at(place), :].astype(F32)


def relay_kernel(*refs):
    pairs, (dense, got, acc) = refs[:-3], refs[-3:]
    read_tags(pairs, acc.shape[0], got)
    acc[...] = jnp.zeros(acc.shape, F32)
    add_pairs(pairs, got, acc)
    dense[...] = acc[...].astype(BF16)


def project(block, mean, feat, w_self, w_neigh, at, shares):
    width = shares[0].shape[1]
    value = dot_nn(feat[block], w_self[...]) + dot_nn(mean, w_neigh[...])
    value = value.astype(BF16)
    for piece, share in enumerate(shares):
        share[at, :] = value[:, piece * width : (piece + 1) * width]


def mid_kernel(half, shards, *refs):
    pairs, rest = refs[:half], refs[half:]
    dense, local, feat, w_self, w_neigh, degrees, averaged, later = rest[:8]
    shares, (got, acc) = rest[8 : 8 + shards], rest[8 + shards :]
    read_tags(pairs, acc.shape[0], got)
    acc[...] = local[...] + dense[...].astype(F32)
    add_pairs(pairs, got, acc)
    divisor = degree_columns(degrees)
    count = averaged.shape[0] // TILE
    for block in range(count):
        at = block_at(block)
        mean = (acc[block] / divisor[:, block : block + 1]).astype(BF16)
        averaged[at, :] = mean
        project(block, mean, feat, w_self, w_neigh, at, shares)
    later[...] = acc[count:]


def later_mid_kernel(sums, feat, w_self, w_neigh, degrees, averaged, *shares):
    divisor = degree_columns(degrees)
    first = feat.shape[0] - sums.shape[0]
    for place in range(sums.shape[0]):
        block, at = first + place, block_at(place)
        mean = (sums[place] / divisor[:, block : block + 1]).astype(BF16)
        averaged[at, :] = mean
        project(block, mean, feat, w_self, w_neigh, at, shares)


def value_and_gate(shares, at):
    value = shares[0][at, :].astype(F32)
    for piece in shares[1:]:
        value = value + piece[at, :].astype(F32)
    return value, 1.0 / (1.0 + jnp.exp(-value))


def slopes_kernel(first, *refs):
    shares, cotangent, slopes = refs[:-2], refs[-2], refs[-1]
    for block in range(slopes.shape[0] // TILE):
        at = block_at(block)
        value, gate = value_and_gate(shares, at)
        slope = gate * (1.0 + value * (1.0 - gate))
        slopes[at, :] = (cotangent[block_at(first + block), :].astype(F32) * slope).astype(BF16)


def output_kernel(*refs):
    shares, output = refs[:-1], refs[-1]
    first, second = shares[: len(shares) // 2], shares[len(shares) // 2 :]
    count = first[0].shape[0] // TILE
    for block in range(output.shape[0] // TILE):
        value, gate = value_and_gate(second if block >= count else first, block_at(block % count))
        output[block_at(block), :] = (value * gate).astype(BF16)


def slopes_times(slopes, weights, at):
    width = slopes[0].shape[1]
    total = dot_nt(slopes[0][at, :], weights[:, :width])
    for piece in range(1, len(slopes)):
        columns = slice(piece * width, (piece + 1) * width)
        total = total + dot_nt(slopes[piece][at, :], weights[:, columns])
    return total


def back_kernel(first, w_neigh, degrees, *refs):
    slopes, back = refs[:-1], refs[-1]
    divisor = degree_columns(degrees)
    for place in range(back.shape[0]):
        block = first + place
        total = slopes_times(slopes, w_neigh, block_at(place))
        back[place] = (total / divisor[:, block : block + 1]).astype(BF16)


def with_block(chunks, block, action):
    count = chunks[0].shape[0]
    for number, chunk in enumerate(chunks):
        first = number * count

        @pl.when((block >= first) & (block < first + count))
        def _():
            action(chunk, block - first)


def spread_kernel(got, first, second, *outs):
    for number, out in enumerate(outs, 1):
        for place in range(CAP):

            def copy(chunk, block):
                out[block_at(place), :] = chunk[block]

            with_block((first, second), got[number * CAP + place], copy)


def grads_kernel(inner, feat, means, more_means, *refs):
    shards = lax.axis_size("chan")
    chunks, outs, whole = refs[: 2 * shards], refs[2 * shards : -1], refs[-1]
    channels = feat.shape[1]
    count, width = chunks[0].shape
    for piece in range(shards):
        columns = slice(piece * width, (piece + 1) * width)
        first, second = chunks[piece][...], chunks[shards + piece][...]
        whole[:channels, columns] = dot_tn(feat[:count, :], first) + dot_tn(
            feat[count:, :], second
        )
        whole[channels:, columns] = dot_tn(means[...], first) + dot_tn(more_means[...], second)
    me = lax.axis_index("dom") & (inner - 1)
    rows = outs[0].shape[0]
    for relative, out in enumerate(outs):
        for owner in range(inner):

            @pl.when((me ^ relative) == owner)
            def _():
                out[...] = whole[owner * rows : (owner + 1) * rows, :].astype(out.dtype)


def gather_sum_kernel(*refs):
    parts, out = refs[:-1], refs[-1]
    total = parts[0][...].astype(F32)
    for part in parts[1:]:
        total = total + part[...].astype(F32)
    out[...] = total.astype(BF16)


def place_rows(parts, out):
    me = lax.axis_index("dom") & (len(parts) - 1)
    rows = parts[0].shape[0]
    for relative, part in enumerate(parts):
        for owner in range(len(parts)):

            @pl.when((me ^ relative) == owner)
            def _():
                out[owner * rows : (owner + 1) * rows, :] = part[...]


def finish_grads_kernel(scale, *refs):
    parts, outs, whole = refs[:-3], refs[-3:-1], refs[-1]
    place_rows(parts, whole)
    shards = lax.axis_size("chan")
    me = lax.axis_index("chan")
    columns = whole.shape[1]
    channels = outs[0].shape[0]
    for own in range(shards):

        @pl.when(me == own)
        def _():
            cut = own * (columns // shards)
            for number, out in enumerate(outs):
                rows = slice(number * channels, (number + 1) * channels)
                out[:, cut:] = whole[rows, : columns - cut].astype(F32) * scale
                if cut:
                    out[:, :cut] = whole[rows, columns - cut :].astype(F32) * scale


def local_back_kernel(shards, src, dst, tiles, first, second, w_self, *refs):
    chunks, out, back = refs[: 2 * shards], refs[2 * shards], refs[2 * shards + 1]
    count = first.shape[0]
    back[:count] = first[...]
    back[count:] = second[...]
    for block in range(out.shape[0]):
        slopes = chunks[shards:] if block >= count else chunks[:shards]
        out[block] = slopes_times(slopes, w_self, block_at(block % count))
    for number in range(tiles.shape[0]):
        out[src[number]] += dot_nn(tiles[number], back[dst[number]])


def final_kernel(half, src, dst, slots, tiles, *refs):
    back, far, partial = refs[:2], refs[2:4], refs[4]
    near_rows, far_rows = refs[5 : half + 4], refs[half + 4 : 2 * half + 3]
    out, rows, acc = refs[2 * half + 3 :]
    me = lax.axis_index("dom")
    for relative in range(2 * half):
        target = me ^ relative
        shift = relative % half
        for place in range(CAP):
            number = slots[target * CAP + place]
            if shift:
                arrived = (near_rows if relative < half else far_rows)[shift - 1]

                @pl.when(number >= 0)
                def _():
                    rows[number] = arrived[block_at(place), :]
            else:
                held = jnp.where(number >= 0, dst[jnp.maximum(number, 0)], -1)

                def copy(chunk, block):
                    rows[number] = chunk[block]

                with_block(back if relative < half else far, held, copy)

    acc[...] = partial[...]
    for number in range(tiles.shape[0]):
        acc[src[number]] += dot_nn(tiles[number], rows[number])
    out[...] = acc[...].astype(BF16)


def swap(value, relative):
    count = lax.axis_size("dom")
    pairs = [(at, at ^ relative) for at in range(count)]
    return lax.ppermute(value, "dom", pairs)


def nearest_first(top, bottom=1):
    return sorted(range(bottom, top), key=lambda k: (k.bit_count(), -k))


def swap_all(values, first):
    out = [values[0]] + [None] * (len(values) - 1)
    for k in nearest_first(len(values)):
        out[k] = swap(values[k], k * first)
    return out


def around(value, shift):
    count = lax.axis_size("chan")
    pairs = [(at, (at + shift) % count) for at in range(count)]
    return lax.ppermute(value, "chan", pairs)


def per_device(
    features,
    w_self,
    w_neigh,
    degrees,
    local_src,
    local_dst,
    local_tiles,
    remote_src,
    remote_part,
    remote_dst,
    remote_tiles,
    cotangent,
):
    domains = lax.axis_size("dom")
    shards = lax.axis_size("chan")
    node_rows, channels = features.shape
    out_width = w_self.shape[1]
    own_width = out_width // shards
    blocks = node_rows // TILE
    n_remote = remote_tiles.shape[0]
    half = domains // 2
    early = max(1, half // 2)
    inner, outer_bits = inner_and_outer(domains)
    feat_blocks = features.reshape(blocks, TILE, channels)
    degree_rows = degrees.reshape(blocks, TILE)
    targets = remote_part[:, 0]
    block_shape = (blocks, TILE, channels)
    product_shape = (n_remote, TILE, channels)
    pair_shape = shape((PAIR + TAG_ROWS, channels), BF16)
    slot_shape = shape((domains * CAP,), I32)
    got_shape = shape((half * CAP,), I32)

    pushed = call(
        lambda *refs: push_far_kernel(half, *refs),
        [(VMEM, pair_shape)] * half
        + [(VMEM, shape(product_shape, BF16)), (SMEM, slot_shape), (SMEM, slot_shape)],
        [(HBM, a) for a in (remote_src, targets, remote_dst, feat_blocks, remote_tiles)],
        [pltpu.SMEM((n_remote,), I32)] * 3
        + [
            pltpu.VMEM(block_shape, BF16),
            pltpu.VMEM(remote_tiles.shape, BF16),
            pltpu.SMEM((domains,), I32),
            pltpu.SemaphoreType.DMA((5,)),
        ],
        limit=None,
    )
    far, (product, slots, tags) = pushed[:half], pushed[half:]
    relayed = swap_all(far, 1)
    near = call(
        push_near_kernel, [(VMEM, pair_shape)] * half, vmem([product]) + smem([slots, tags])
    )
    (local,) = call(
        local_kernel,
        [(VMEM, shape(block_shape, F32))],
        smem([local_src, local_dst]) + vmem([feat_blocks, local_tiles]),
    )
    own_self, own_neigh = call(
        rotate_kernel, [(VMEM, shape(w_self.shape, BF16))] * 2, vmem([w_self, w_neigh])
    )
    dense, got_far = call(
        relay_kernel,
        [(VMEM, shape(block_shape, BF16)), (SMEM, got_shape)],
        vmem(relayed),
        [pltpu.VMEM(block_shape, F32)],
    )
    crossed = swap(dense, half)
    direct = [near[0]] + [None] * (half - 1)
    for k in [*nearest_first(half, early), *nearest_first(early)]:
        direct[k] = swap(near[k], k)

    chunk_blocks = (blocks // 2, blocks - blocks // 2)
    chunk_rows = chunk_blocks[0] * TILE
    share_shape = shape((chunk_rows, own_width), BF16)
    mean_shape = shape((chunk_rows, channels), BF16)
    means, later, *shares, got_near = call(
        lambda *refs: mid_kernel(half, shards, *refs),
        [(VMEM, mean_shape), (VMEM, shape((chunk_blocks[1], TILE, channels), F32))]
        + [(VMEM, share_shape)] * shards
        + [(SMEM, got_shape)],
        vmem(direct + [crossed, local, feat_blocks, own_self, own_neigh, degree_rows]),
        [pltpu.VMEM(block_shape, F32)],
    )
    more_means, *more_shares = call(
        later_mid_kernel,
        [(VMEM, mean_shape)] + [(VMEM, share_shape)] * shards,
        vmem([later, feat_blocks, own_self, own_neigh, degree_rows]),
    )
    pieces, slopes, back, back_far = [], [], [], []
    for chunk, part in enumerate((shares, more_shares)):
        arrived = [around(part[k], k) for k in range(1, shards)]
        pieces += [part[0], *arrived]
    for chunk in range(2):
        (own,) = call(
            lambda *refs: slopes_kernel(chunk * chunk_blocks[0], *refs),
            [(VMEM, share_shape)],
            vmem(pieces[chunk * shards : (chunk + 1) * shards] + [cotangent]),
        )
        slopes += [own] + [around(own, shards - k) for k in range(1, shards)]
    for chunk in range(2):
        (rows,) = call(
            lambda *refs: back_kernel(chunk * chunk_blocks[0], *refs),
            [(VMEM, shape((chunk_blocks[chunk], TILE, channels), BF16))],
            vmem([own_neigh, degree_rows] + slopes[chunk * shards : (chunk + 1) * shards]),
        )
        back.append(rows)
        back_far.append(swap(rows, half))
    returning = shape((PAIR, channels), BF16)
    near_out = call(spread_kernel, [(VMEM, returning)] * (half - 1), smem([got_near]) + vmem(back))
    near_back = swap_all([None, *near_out], 1)[1:]

    rows_inner = 2 * channels // inner
    terms = call(
        lambda *refs: grads_kernel(inner, *refs),
        [(VMEM, shape((rows_inner, out_width), F32))]
        + [(VMEM, shape((rows_inner, out_width), BF16))] * (inner - 1),
        vmem([features, means, more_means] + slopes),
        [pltpu.VMEM((2 * channels, out_width), F32)],
    )
    part_shape = shape((rows_inner, out_width), BF16)
    (total,) = call(gather_sum_kernel, [(VMEM, part_shape)], vmem(swap_all(terms, 1)))
    for bit in range(outer_bits):
        arrived = swap(total, inner << bit)
        (total,) = call(gather_sum_kernel, [(VMEM, part_shape)], vmem([total, arrived]))
    totals = swap_all([total] * inner, 1)
    scale = 1.0 / math.sqrt(float(node_rows * domains))
    grad_self, grad_neigh = call(
        lambda *refs: finish_grads_kernel(scale, *refs),
        [(VMEM, shape((channels, out_width), F32))] * 2,
        vmem(totals),
        [pltpu.VMEM((2 * channels, out_width), BF16)],
    )

    far_out = call(
        spread_kernel, [(VMEM, returning)] * (half - 1), smem([got_far]) + vmem(back_far)
    )
    far_back = swap_all([None, *far_out], 1)[1:]
    (partial,) = call(
        lambda *refs: local_back_kernel(shards, *refs),
        [(VMEM, shape(block_shape, F32))],
        smem([local_src, local_dst]) + vmem([local_tiles, *back, own_self] + slopes),
        [pltpu.VMEM(block_shape, BF16)],
    )
    (output,) = call(output_kernel, [(VMEM, shape((node_rows, own_width), BF16))], vmem(pieces))
    (grad_features,) = call(
        lambda *refs: final_kernel(half, *refs),
        [(VMEM, shape(block_shape, BF16))],
        smem([remote_src, remote_dst, slots])
        + vmem([remote_tiles, *back, *back_far, partial] + near_back + far_back),
        [pltpu.VMEM(product_shape, BF16), pltpu.VMEM(block_shape, F32)],
    )
    return (output, grad_self, grad_neigh, grad_features.reshape(node_rows, channels))


def inner_and_outer(domains):
    inner_bits = domains.bit_length() // 2
    return 1 << inner_bits, domains.bit_length() - 1 - inner_bits


def solution(mesh):
    in_specs = (
        P("dom", "chan"),
        P("chan", None),
        P("chan", None),
        P("dom"),
        P("dom"),
        P("dom"),
        P("dom", None, None),
        P("dom"),
        P("dom", None),
        P("dom"),
        P("dom", None, None),
        P("dom", "chan"),
    )
    out_specs = (P("dom", "chan"), P("chan", None), P("chan", None), P("dom", "chan"))
    return jax.shard_map(
        per_device, mesh=mesh, in_specs=in_specs, out_specs=out_specs, check_vma=False
    )
```

```python
import math

import jax
import jax.numpy as jnp
from jax import lax
from jax.experimental import pallas as pl
from jax.experimental.pallas import tpu as pltpu
from jax.sharding import PartitionSpec as P


TILE = 128
CAP = 2
TAG_ROWS = 8
PAIR = CAP * TILE

F32 = jnp.float32
BF16 = jnp.bfloat16
I32 = jnp.int32
VMEM = pl.BlockSpec(memory_space=pltpu.VMEM)
SMEM = pl.BlockSpec(memory_space=pltpu.SMEM)
HBM = pl.BlockSpec(memory_space=pltpu.HBM)


def shape(dims, dtype):
    return jax.ShapeDtypeStruct(dims, dtype)


def call(kernel, outs, ins, scratch=(), flops=1 << 20, limit=16 * 1024 * 1024, nbytes=1 << 20):
    return pl.pallas_call(
        kernel,
        out_shape=tuple(out for _, out in outs),
        in_specs=[spec for spec, _ in ins],
        out_specs=tuple(spec for spec, _ in outs),
        scratch_shapes=list(scratch),
        compiler_params=pltpu.CompilerParams(vmem_limit_bytes=limit),
        cost_estimate=pl.CostEstimate(flops=flops, bytes_accessed=nbytes, transcendentals=0),
    )(*[array for _, array in ins])


def vmem(arrays):
    return [(VMEM, array) for array in arrays]


def smem(arrays):
    return [(SMEM, array) for array in arrays]


def dot_tn(a, b):
    return lax.dot_general(a, b, (((0,), (0,)), ((), ())), preferred_element_type=F32)


def dot_nn(a, b):
    return lax.dot_general(a, b, (((1,), (0,)), ((), ())), preferred_element_type=F32)


def dot_nt(a, b):
    return lax.dot_general(a, b, (((1,), (1,)), ((), ())), preferred_element_type=F32)


def block_at(number):
    return slice(number * TILE, (number + 1) * TILE)


def fill_slots(part, count, slots, tiles):
    for place in range(count.shape[0]):
        count[place] = 0
    for place in range(slots.shape[0]):
        slots[place] = -1
    for number in range(tiles):
        target = part[number]
        place = count[target]
        count[target] = place + 1
        slots[target * CAP + place] = number


def degree_columns(degrees):
    return jnp.transpose(degrees[...].astype(F32))


def place_tiles(outs, first, product, slots, tags):
    me = lax.axis_index("dom")
    row_at = lax.broadcasted_iota(I32, (TAG_ROWS, product.shape[2]), 0)
    for relative, out in enumerate(outs, first):
        target = me ^ relative
        marks = jnp.zeros((TAG_ROWS, product.shape[2]), F32)
        for place in range(CAP):
            number = slots[target * CAP + place]
            marks = jnp.where(row_at == place, tags[target * CAP + place].astype(F32), marks)

            @pl.when(number >= 0)
            def _():
                out[block_at(place), :] = product[number]

        out[PAIR:, :] = marks.astype(BF16)


def push_far_kernel(half, src_hbm, part_hbm, dst_hbm, feat_hbm, tiles_hbm, *refs):
    outs, (product, slots, tags) = refs[:half], refs[half : half + 3]
    src, part, dst, feat, tiles, count, sems = refs[half + 3 :]
    pairs = [
        (part_hbm, part),
        (dst_hbm, dst),
        (src_hbm, src),
        (feat_hbm, feat),
        (tiles_hbm, tiles),
    ]
    copies = [
        pltpu.make_async_copy(source, target, sems.at[number])
        for number, (source, target) in enumerate(pairs)
    ]
    for copy in copies:
        copy.start()
    copies[0].wait()
    copies[1].wait()
    fill_slots(part, count, slots, tiles.shape[0])
    for place in range(slots.shape[0]):
        number = slots[place]
        tags[place] = jnp.where(number >= 0, dst[jnp.maximum(number, 0)] + 1, 0)
    for copy in copies[2:]:
        copy.wait()
    for number in range(tiles.shape[0]):
        product[number] = dot_tn(tiles[number], feat[src[number]]).astype(BF16)
    place_tiles(outs, half, product, slots, tags)


def push_near_kernel(product, slots, tags, *outs):
    place_tiles(outs, 0, product, slots, tags)


def local_kernel(src, dst, feat, tiles, out):
    out[...] = jnp.zeros(out.shape, F32)
    for number in range(tiles.shape[0]):
        out[dst[number]] += dot_tn(tiles[number], feat[src[number]])


def rotate_kernel(first, second, out_first, out_second):
    shards = lax.axis_size("chan")
    me = lax.axis_index("chan")
    width = first.shape[1] // shards
    for own in range(shards):

        @pl.when(me == own)
        def _():
            cut = own * width
            for source, out in ((first, out_first), (second, out_second)):
                out[:, : source.shape[1] - cut] = source[:, cut:]
                if cut:
                    out[:, source.shape[1] - cut :] = source[:, :cut]


def read_tags(pairs, blocks, got):
    channels = pairs[0].shape[1]
    bits = blocks.bit_length()
    per_word = max(1, 24 // (bits * CAP))
    row_at = lax.broadcasted_iota(I32, (TAG_ROWS, channels), 0)
    unit = jnp.zeros((TAG_ROWS, channels), F32)
    for place in range(CAP):
        unit = jnp.where(row_at == place, float(1 << (bits * place)), unit)
    for first in range(0, len(pairs), per_word):
        members = range(first, min(first + per_word, len(pairs)))
        word = jnp.zeros((TAG_ROWS, channels), F32)
        for member in members:
            scale = float(1 << (bits * CAP * (member - first)))
            word = word + pairs[member][PAIR:, :].astype(F32) * (unit * scale)
        packed = jnp.max(jnp.sum(word, axis=0, keepdims=True)).astype(I32)
        for member in members:
            for place in range(CAP):
                shift = bits * (CAP * (member - first) + place)
                got[member * CAP + place] = ((packed >> shift) & (2**bits - 1)) - 1


def add_pairs(pairs, got, acc):
    for number, pair in enumerate(pairs):
        for place in range(CAP):
            block = got[number * CAP + place]

            @pl.when(block >= 0)
            def _():
                acc[block] += pair[block_at(place), :].astype(F32)


def relay_kernel(*refs):
    pairs, (dense, more_dense, got, acc) = refs[:-4], refs[-4:]
    read_tags(pairs, acc.shape[0], got)
    acc[...] = jnp.zeros(acc.shape, F32)
    add_pairs(pairs, got, acc)
    count = dense.shape[0]
    dense[...] = acc[:count].astype(BF16)
    more_dense[...] = acc[count:].astype(BF16)


def project(block, mean, feat, w_self, w_neigh, at, shares):
    width = shares[0].shape[1]
    value = dot_nn(feat[block], w_self[...]) + dot_nn(mean, w_neigh[...])
    value = value.astype(BF16)
    for piece, share in enumerate(shares):
        share[at, :] = value[:, piece * width : (piece + 1) * width]


def mid_kernel(half, shards, *refs):
    pairs, rest = refs[:half], refs[half:]
    dense, local, feat, w_self, w_neigh, degrees, averaged, later = rest[:8]
    shares, (got, acc) = rest[8 : 8 + shards], rest[8 + shards :]
    read_tags(pairs, acc.shape[0], got)
    count = dense.shape[0]
    acc[:count] = local[:count] + dense[...].astype(F32)
    acc[count:] = local[count:]
    add_pairs(pairs, got, acc)
    divisor = degree_columns(degrees)
    for block in range(count):
        at = block_at(block)
        mean = (acc[block] / divisor[:, block : block + 1]).astype(BF16)
        averaged[at, :] = mean
        project(block, mean, feat, w_self, w_neigh, at, shares)
    later[...] = acc[count:]


def later_mid_kernel(sums, dense, feat, w_self, w_neigh, degrees, averaged, *shares):
    divisor = degree_columns(degrees)
    first = feat.shape[0] - sums.shape[0]
    for place in range(sums.shape[0]):
        block, at = first + place, block_at(place)
        total = sums[place] + dense[place].astype(F32)
        mean = (total / divisor[:, block : block + 1]).astype(BF16)
        averaged[at, :] = mean
        project(block, mean, feat, w_self, w_neigh, at, shares)


def value_and_gate(shares, at):
    value = shares[0][at, :].astype(F32)
    for piece in shares[1:]:
        value = value + piece[at, :].astype(F32)
    return value, 1.0 / (1.0 + jnp.exp(-value))


def slopes_kernel(first, *refs):
    shares, cotangent, slopes = refs[:-2], refs[-2], refs[-1]
    for block in range(slopes.shape[0] // TILE):
        at = block_at(block)
        value, gate = value_and_gate(shares, at)
        slope = gate * (1.0 + value * (1.0 - gate))
        slopes[at, :] = (cotangent[block_at(first + block), :].astype(F32) * slope).astype(BF16)


def output_kernel(*refs):
    shares, output = refs[:-1], refs[-1]
    first, second = shares[: len(shares) // 2], shares[len(shares) // 2 :]
    count = first[0].shape[0] // TILE
    for block in range(output.shape[0] // TILE):
        value, gate = value_and_gate(second if block >= count else first, block_at(block % count))
        output[block_at(block), :] = (value * gate).astype(BF16)


def slopes_times(slopes, weights, at):
    width = slopes[0].shape[1]
    total = dot_nt(slopes[0][at, :], weights[:, :width])
    for piece in range(1, len(slopes)):
        columns = slice(piece * width, (piece + 1) * width)
        total = total + dot_nt(slopes[piece][at, :], weights[:, columns])
    return total


def back_kernel(first, w_neigh, degrees, *refs):
    slopes, back = refs[:-1], refs[-1]
    divisor = degree_columns(degrees)
    for place in range(back.shape[0]):
        block = first + place
        total = slopes_times(slopes, w_neigh, block_at(place))
        back[place] = (total / divisor[:, block : block + 1]).astype(BF16)


def with_block(chunks, block, action):
    count = chunks[0].shape[0]
    for number, chunk in enumerate(chunks):
        first = number * count

        @pl.when((block >= first) & (block < first + count))
        def _():
            action(chunk, block - first)


def spread_kernel(got, first, second, *outs):
    for number, out in enumerate(outs, 1):
        for place in range(CAP):

            def copy(chunk, block):
                out[block_at(place), :] = chunk[block]

            with_block((first, second), got[number * CAP + place], copy)


def grads_kernel(inner, feat, means, more_means, *refs):
    shards = lax.axis_size("chan")
    chunks, outs, whole = refs[: 2 * shards], refs[2 * shards : -1], refs[-1]
    channels = feat.shape[1]
    count, width = chunks[0].shape
    for piece in range(shards):
        columns = slice(piece * width, (piece + 1) * width)
        first, second = chunks[piece][...], chunks[shards + piece][...]
        whole[:channels, columns] = dot_tn(feat[:count, :], first) + dot_tn(
            feat[count:, :], second
        )
        whole[channels:, columns] = dot_tn(means[...], first) + dot_tn(more_means[...], second)
    me = lax.axis_index("dom") & (inner - 1)
    rows = outs[0].shape[0]
    for relative, out in enumerate(outs):
        for owner in range(inner):

            @pl.when((me ^ relative) == owner)
            def _():
                out[...] = whole[owner * rows : (owner + 1) * rows, :].astype(out.dtype)


def gather_sum_kernel(*refs):
    parts, out = refs[:-1], refs[-1]
    total = parts[0][...].astype(F32)
    for part in parts[1:]:
        total = total + part[...].astype(F32)
    out[...] = total.astype(BF16)


def place_rows(parts, out):
    me = lax.axis_index("dom") & (len(parts) - 1)
    rows = parts[0].shape[0]
    for relative, part in enumerate(parts):
        for owner in range(len(parts)):

            @pl.when((me ^ relative) == owner)
            def _():
                out[owner * rows : (owner + 1) * rows, :] = part[...]


def finish_grads_kernel(scale, *refs):
    parts, outs, whole = refs[:-3], refs[-3:-1], refs[-1]
    place_rows(parts, whole)
    shards = lax.axis_size("chan")
    me = lax.axis_index("chan")
    columns = whole.shape[1]
    channels = outs[0].shape[0]
    for own in range(shards):

        @pl.when(me == own)
        def _():
            cut = own * (columns // shards)
            for number, out in enumerate(outs):
                rows = slice(number * channels, (number + 1) * channels)
                out[:, cut:] = whole[rows, : columns - cut].astype(F32) * scale
                if cut:
                    out[:, :cut] = whole[rows, columns - cut :].astype(F32) * scale


def local_back_kernel(shards, src, dst, tiles, first, second, w_self, *refs):
    chunks, out, back = refs[: 2 * shards], refs[2 * shards], refs[2 * shards + 1]
    count = first.shape[0]
    back[:count] = first[...]
    back[count:] = second[...]
    for block in range(out.shape[0]):
        slopes = chunks[shards:] if block >= count else chunks[:shards]
        out[block] = slopes_times(slopes, w_self, block_at(block % count))
    for number in range(tiles.shape[0]):
        out[src[number]] += dot_nn(tiles[number], back[dst[number]])


def final_kernel(half, src, dst, slots, tiles, *refs):
    back, far, partial = refs[:2], refs[2:4], refs[4]
    near_rows, far_rows = refs[5 : half + 4], refs[half + 4 : 2 * half + 3]
    out, rows, acc = refs[2 * half + 3 :]
    me = lax.axis_index("dom")
    for relative in range(2 * half):
        target = me ^ relative
        shift = relative % half
        for place in range(CAP):
            number = slots[target * CAP + place]
            if shift:
                arrived = (near_rows if relative < half else far_rows)[shift - 1]

                @pl.when(number >= 0)
                def _():
                    rows[number] = arrived[block_at(place), :]
            else:
                held = jnp.where(number >= 0, dst[jnp.maximum(number, 0)], -1)

                def copy(chunk, block):
                    rows[number] = chunk[block]

                with_block(back if relative < half else far, held, copy)

    acc[...] = partial[...]
    for number in range(tiles.shape[0]):
        acc[src[number]] += dot_nn(tiles[number], rows[number])
    out[...] = acc[...].astype(BF16)


def swap(value, relative):
    count = lax.axis_size("dom")
    pairs = [(at, at ^ relative) for at in range(count)]
    return lax.ppermute(value, "dom", pairs)


def nearest_first(top, bottom=1):
    return sorted(range(bottom, top), key=lambda k: (k.bit_count(), -k))


def swap_all(values, first):
    out = [values[0]] + [None] * (len(values) - 1)
    for k in nearest_first(len(values)):
        out[k] = swap(values[k], k * first)
    return out


def around(value, shift):
    count = lax.axis_size("chan")
    pairs = [(at, (at + shift) % count) for at in range(count)]
    return lax.ppermute(value, "chan", pairs)


def per_device(
    features,
    w_self,
    w_neigh,
    degrees,
    local_src,
    local_dst,
    local_tiles,
    remote_src,
    remote_part,
    remote_dst,
    remote_tiles,
    cotangent,
):
    domains = lax.axis_size("dom")
    shards = lax.axis_size("chan")
    node_rows, channels = features.shape
    out_width = w_self.shape[1]
    own_width = out_width // shards
    blocks = node_rows // TILE
    n_remote = remote_tiles.shape[0]
    half = domains // 2
    early = max(1, half // 2)
    inner, outer_bits = inner_and_outer(domains)
    feat_blocks = features.reshape(blocks, TILE, channels)
    degree_rows = degrees.reshape(blocks, TILE)
    targets = remote_part[:, 0]
    block_shape = (blocks, TILE, channels)
    product_shape = (n_remote, TILE, channels)
    pair_shape = shape((PAIR + TAG_ROWS, channels), BF16)
    slot_shape = shape((domains * CAP,), I32)
    got_shape = shape((half * CAP,), I32)

    pushed = call(
        lambda *refs: push_far_kernel(half, *refs),
        [(VMEM, pair_shape)] * half
        + [(VMEM, shape(product_shape, BF16)), (SMEM, slot_shape), (SMEM, slot_shape)],
        [(HBM, a) for a in (remote_src, targets, remote_dst, feat_blocks, remote_tiles)],
        [pltpu.SMEM((n_remote,), I32)] * 3
        + [
            pltpu.VMEM(block_shape, BF16),
            pltpu.VMEM(remote_tiles.shape, BF16),
            pltpu.SMEM((domains,), I32),
            pltpu.SemaphoreType.DMA((5,)),
        ],
        limit=None,
    )
    far, (product, slots, tags) = pushed[:half], pushed[half:]
    relayed = swap_all(far, 1)
    near = call(
        push_near_kernel, [(VMEM, pair_shape)] * half, vmem([product]) + smem([slots, tags])
    )
    (local,) = call(
        local_kernel,
        [(VMEM, shape(block_shape, F32))],
        smem([local_src, local_dst]) + vmem([feat_blocks, local_tiles]),
    )
    own_self, own_neigh = call(
        rotate_kernel, [(VMEM, shape(w_self.shape, BF16))] * 2, vmem([w_self, w_neigh])
    )
    chunk_blocks = (blocks // 2, blocks - blocks // 2)
    chunk_shapes = [(VMEM, shape((count, TILE, channels), BF16)) for count in chunk_blocks]
    dense, more_dense, got_far = call(
        relay_kernel,
        [*chunk_shapes, (SMEM, got_shape)],
        vmem(relayed),
        [pltpu.VMEM(block_shape, F32)],
    )
    crossed = swap(dense, half)
    more_crossed = swap(more_dense, half)
    direct = [near[0]] + [None] * (half - 1)
    for k in [*nearest_first(half, early), *nearest_first(early)]:
        direct[k] = swap(near[k], k)

    chunk_rows = chunk_blocks[0] * TILE
    share_shape = shape((chunk_rows, own_width), BF16)
    mean_shape = shape((chunk_rows, channels), BF16)
    means, later, *shares, got_near = call(
        lambda *refs: mid_kernel(half, shards, *refs),
        [(VMEM, mean_shape), (VMEM, shape((chunk_blocks[1], TILE, channels), F32))]
        + [(VMEM, share_shape)] * shards
        + [(SMEM, got_shape)],
        vmem(direct + [crossed, local, feat_blocks, own_self, own_neigh, degree_rows]),
        [pltpu.VMEM(block_shape, F32)],
    )
    more_means, *more_shares = call(
        later_mid_kernel,
        [(VMEM, mean_shape)] + [(VMEM, share_shape)] * shards,
        vmem([later, more_crossed, feat_blocks, own_self, own_neigh, degree_rows]),
    )
    pieces, slopes, back, back_far = [], [], [], []
    for chunk, part in enumerate((shares, more_shares)):
        arrived = [around(part[k], k) for k in range(1, shards)]
        pieces += [part[0], *arrived]
    for chunk in range(2):
        (own,) = call(
            lambda *refs: slopes_kernel(chunk * chunk_blocks[0], *refs),
            [(VMEM, share_shape)],
            vmem(pieces[chunk * shards : (chunk + 1) * shards] + [cotangent]),
        )
        slopes += [own] + [around(own, shards - k) for k in range(1, shards)]
    for chunk in range(2):
        (rows,) = call(
            lambda *refs: back_kernel(chunk * chunk_blocks[0], *refs),
            [(VMEM, shape((chunk_blocks[chunk], TILE, channels), BF16))],
            vmem([own_neigh, degree_rows] + slopes[chunk * shards : (chunk + 1) * shards]),
        )
        back.append(rows)
        back_far.append(swap(rows, half))
    returning = shape((PAIR, channels), BF16)
    near_out = call(spread_kernel, [(VMEM, returning)] * (half - 1), smem([got_near]) + vmem(back))
    near_back = swap_all([None, *near_out], 1)[1:]

    rows_inner = 2 * channels // inner
    terms = call(
        lambda *refs: grads_kernel(inner, *refs),
        [(VMEM, shape((rows_inner, out_width), F32))]
        + [(VMEM, shape((rows_inner, out_width), BF16))] * (inner - 1),
        vmem([features, means, more_means] + slopes),
        [pltpu.VMEM((2 * channels, out_width), F32)],
    )
    part_shape = shape((rows_inner, out_width), BF16)
    (total,) = call(gather_sum_kernel, [(VMEM, part_shape)], vmem(swap_all(terms, 1)))
    for bit in range(outer_bits):
        arrived = swap(total, inner << bit)
        (total,) = call(gather_sum_kernel, [(VMEM, part_shape)], vmem([total, arrived]))
    totals = swap_all([total] * inner, 1)
    scale = 1.0 / math.sqrt(float(node_rows * domains))
    grad_self, grad_neigh = call(
        lambda *refs: finish_grads_kernel(scale, *refs),
        [(VMEM, shape((channels, out_width), F32))] * 2,
        vmem(totals),
        [pltpu.VMEM((2 * channels, out_width), BF16)],
    )

    far_out = call(
        spread_kernel, [(VMEM, returning)] * (half - 1), smem([got_far]) + vmem(back_far)
    )
    far_back = swap_all([None, *far_out], 1)[1:]
    (partial,) = call(
        lambda *refs: local_back_kernel(shards, *refs),
        [(VMEM, shape(block_shape, F32))],
        smem([local_src, local_dst]) + vmem([local_tiles, *back, own_self] + slopes),
        [pltpu.VMEM(block_shape, BF16)],
    )
    (output,) = call(output_kernel, [(VMEM, shape((node_rows, own_width), BF16))], vmem(pieces))
    (grad_features,) = call(
        lambda *refs: final_kernel(half, *refs),
        [(VMEM, shape(block_shape, BF16))],
        smem([remote_src, remote_dst, slots])
        + vmem([remote_tiles, *back, *back_far, partial] + near_back + far_back),
        [pltpu.VMEM(product_shape, BF16), pltpu.VMEM(block_shape, F32)],
    )
    return (output, grad_self, grad_neigh, grad_features.reshape(node_rows, channels))


def inner_and_outer(domains):
    inner_bits = domains.bit_length() // 2
    return 1 << inner_bits, domains.bit_length() - 1 - inner_bits


def solution(mesh):
    in_specs = (
        P("dom", "chan"),
        P("chan", None),
        P("chan", None),
        P("dom"),
        P("dom"),
        P("dom"),
        P("dom", None, None),
        P("dom"),
        P("dom", None),
        P("dom"),
        P("dom", None, None),
        P("dom", "chan"),
    )
    out_specs = (P("dom", "chan"), P("chan", None), P("chan", None), P("dom", "chan"))
    return jax.shard_map(
        per_device, mesh=mesh, in_specs=in_specs, out_specs=out_specs, check_vma=False
    )
```
